128 devices in a mesh: strike: 16 (over x, z), dip: 8 (over y, core).
Axes of the slice: x: 4, y: 4, z: 4, core: 2. Of those that a mesh axis runs over, the one named last changes fastest.
Arguments:
- pressure: float32 [64, 1024, 1024], P(None, 'strike', 'dip'), may hold values from -6 to 6
- strike_vel: float32 [64, 1024, 1024], P(None, 'strike', 'dip'), may hold values from -6 to 6
- dip_vel: float32 [64, 1024, 1024], P(None, 'strike', 'dip'), may hold values from -6 to 6
- bathy_class: int32 [1024, 1024], P('strike', 'dip'), may hold values from 0 to 7
- bulk_table: float32 [8], replicated, may hold values from 0.5 to 2
- buoy_table: float32 [8], replicated, may hold values from 0.5 to 2
- gravity: float32 [64], replicated, may hold values from 0.5 to 2
- sensor_amp: float32 [4, 1024], P(None, ('strike', 'dip')), may hold values from -12 to 12
- sensor_owner: int32 [1024, 1], P(('strike', 'dip')), may hold values from 0 to 7; in each aligned block of 8 rows (0 to 7, 8 to 15, ...) at most 2 rows name the same one
- sensor_cell: int32 [1024], P(('strike', 'dip')), may hold values from 0 to 8191
- probe_kernel: bfloat16 [96, 1024, 1024], P(None, 'strike', 'dip'), may hold values from -6 to 6
Outputs:
- final_pressure: float32 [64, 1024, 1024], P(None, 'strike', 'dip')
- panel_factor: float32 [96, 96], replicated
The draws below stay inside these ranges and needn't reach their ends.
Inputs may be any that keep to these rules, and one draw needn't show every extreme that they name: `sensor_owner`: the owner lies in the same strike index as the device that holds the sensor; among the 8 sensors of one device at most 2 name the same owner, a bound that some block reaches. `sensor_cell`: numbered row by row within the owner's block, 128 cells a row.
All inputs are finite; a program needn't handle non-finite values.
Results may differ from the reference program's by a relative error of at most 0.0003.
Values sent between devices are 32-bit elements; how exact they have to be, the bound alone decides.
No kernel may reach another device: no remote copies, remote signals or barrier semaphores. Data moves between devices by JAX's collectives and lax.ppermute only.
A program may use at most 128 MiB of HBM per device.

```python
import math
import jax
import jax.numpy as jnp
import numpy as np
from jax import lax

CX = 64
CY = 128
LEV = 64
STEPS = 4
PROBES = 96
NCLASS = 8
S_DEV = 8
CAP = 2
NX = 1024
NY = 1024
SENSORS = 1024
N_STRIKE = 16
N_DIP = 8


def with_ends(entries, own_key, smallest, high):
    extent = entries.shape
    spot = [jax.random.randint(jax.random.fold_in(own_key, axis), (), 0, extent[axis]) for axis in range(len(extent))]
    entries = entries.at[tuple(spot)].set(smallest)
    longest = extent.index(max(extent))
    spot[longest] = (spot[longest] + 1) % extent[longest]
    return entries.at[tuple(spot)].set(high)


def level_of(key, dims, cuts, least, top_value):
    def one(axis_at, parts):
        steps = jax.random.uniform(jax.random.fold_in(jax.random.fold_in(key, 6), axis_at), (parts,), jnp.float32, least / len(cuts), top_value / len(cuts))
        return jnp.repeat(jnp.exp(steps), dims[axis_at] // parts).reshape((-1,) + (1,) * (len(dims) - axis_at - 1))

    factor_of = one(*cuts[0])
    for cut in cuts[1:]:
        factor_of = factor_of * one(*cut)
    return factor_of


def routed_block(stream_key, own, number, rows, amount, top, reach, slope):
    sequence = jax.random.permutation(stream_key, amount)
    packed, ordinary = shares(amount, rows * top, reach, slope, True), shares(amount, rows * top, reach, slope, False)
    places = jnp.arange(amount)

    def named(lengths, rotation):
        used = int((lengths > 0).sum())
        fixed = max(1, used // 4)
        passed = fixed + (places - fixed + rotation * (used - fixed)) % max(1, amount - fixed)
        return jnp.zeros((amount,), jnp.int32).at[sequence[jnp.where(places < fixed, places, passed)]].set(jnp.asarray(lengths, jnp.int32))

    lengths = jnp.where(number % 4 == 0, named(packed, number // 4), named(ordinary, number - number // 4 - 1))
    mixed = jax.random.permutation(jax.random.fold_in(own, 3), amount)
    giver, sink = mixed[0:amount // 2 * 2:2], mixed[1:amount // 2 * 2:2]
    room = jnp.minimum(lengths[giver] - 1, reach - lengths[sink]) // 2
    room = jnp.where((giver == sequence[0]) | (sink == sequence[0]) | (lengths[sink] == 0), 0, jnp.maximum(room, 0))
    passed = jax.random.randint(jax.random.fold_in(own, 4), (amount // 2,), 0, 1 << 20) % (room + 1)
    lengths = lengths.at[giver].add(-passed).at[sink].add(passed)
    items = jnp.searchsorted(jnp.cumsum(lengths), jnp.arange(rows * top), side="right").astype(jnp.int32)
    grid = items.reshape(top, rows).T
    grid = grid[jax.random.permutation(jax.random.fold_in(own, 1), rows)]
    rotation = jax.random.randint(jax.random.fold_in(own, 2), (rows, 1), 0, top)
    return jnp.take_along_axis(grid, (jnp.arange(top)[None, :] + rotation) % top, axis=1)


def shares(count, total, limit, skew, full):
    loads = [(1 << 20) // math.isqrt(standing ** skew) + 1 for standing in range(1, count + 1)]
    largest = limit if full else min(limit, max(-(-total // count), total * loads[0] // sum(loads)))
    least = 1 if total - largest >= count - 1 else 0
    holding, surplus = [largest] + [least] * (count - 1), total - largest - least * (count - 1)
    while surplus > 0:
        free = [i for i in range(1, count) if holding[i] < largest] or [i for i in range(1, count) if holding[i] < limit]
        pool, remaining = sum([loads[i] for i in free]), surplus
        for i in free:
            addition = min(limit - holding[i], max(1, remaining * loads[i] // pool), surplus)
            holding[i] = holding[i] + addition
            surplus = surplus - addition
    return np.array(holding)


def normal_values(own_key, extent, scale, bound, cuts=(), held_as=jnp.bfloat16):
    loudness = level_of(own_key, extent, cuts, -0.22, 0.18) if cuts else 1.0
    values = jax.random.normal(own_key, extent, jnp.float32) * scale * loudness
    return jnp.minimum(jnp.maximum(values, -bound), bound).astype(held_as)


def setup_inputs(seed: int = 0) -> dict:
    keys = jax.random.split(jax.random.key(seed), 12)
    pressure = normal_values(keys[0], (LEV, NX, NY), 1.0, 6.0, ((1, 16), (2, 8)), jnp.float32)
    strike_vel = normal_values(keys[1], (LEV, NX, NY), 1.0, 6.0, ((1, 16), (2, 8)), jnp.float32)
    dip_vel = normal_values(keys[2], (LEV, NX, NY), 1.0, 6.0, ((1, 16), (2, 8)), jnp.float32)
    bathy_class = with_ends(jax.random.randint(keys[3], (NX, NY), 0, NCLASS), jax.random.fold_in(keys[3], 1), 0, NCLASS - 1).astype(jnp.int32)
    bulk_table = jnp.clip(jnp.exp(jax.random.uniform(keys[4], (NCLASS,), jnp.float32, math.log(0.5), math.log(2.0))), 0.5, 2.0)
    buoy_table = jnp.clip(jnp.exp(jax.random.uniform(keys[5], (NCLASS,), jnp.float32, math.log(0.5), math.log(2.0))), 0.5, 2.0)
    gravity = jnp.clip(jnp.exp(jax.random.uniform(keys[6], (LEV,), jnp.float32, math.log(0.5), math.log(2.0))), 0.5, 2.0)
    sensor_amp = normal_values(keys[7], (STEPS, SENSORS), 2.0, 12.0, ((1, 128),), jnp.float32)
    sensor_owner_keys = jax.random.split(jax.random.fold_in(keys[8], 1), SENSORS // S_DEV)
    sensor_owner_turns = jax.random.permutation(jax.random.fold_in(keys[8], 3), SENSORS // S_DEV)
    sensor_owner = jax.vmap(lambda own, number: routed_block(jax.random.fold_in(keys[8], 2), own, number, S_DEV, N_DIP, 1, CAP, 2))(sensor_owner_keys, sensor_owner_turns).reshape((SENSORS, 1))
    sensor_cell = with_ends(jax.random.randint(keys[9], (SENSORS,), 0, CX * CY), jax.random.fold_in(keys[9], 1), 0, (CX * CY) - 1).astype(jnp.int32)
    probe_kernel = normal_values(keys[10], (PROBES, NX, NY), 1.0, 6.0, ((1, 16), (2, 8)))
    return {"pressure": pressure, "strike_vel": strike_vel, "dip_vel": dip_vel, "bathy_class": bathy_class, "bulk_table": bulk_table, "buoy_table": buoy_table, "gravity": gravity, "sensor_amp": sensor_amp, "sensor_owner": sensor_owner, "sensor_cell": sensor_cell, "probe_kernel": probe_kernel}


time_step = 0.2

def fourth_diff(extended, axis):
    length = extended.shape[axis] - 4

    def window(offset):
        return lax.slice_in_dim(extended, offset, offset + length, axis=axis)
    return (8.0 * (window(3) - window(1)) - (window(4) - window(0))) / 12.0

def pad_axis(field, axis, width):
    widths = [(0, 0)] * field.ndim
    widths[axis] = (width, width)
    return jnp.pad(field, widths)

def depth_diff(field):
    padded = pad_axis(field, 0, 1)
    return (padded[2:] - padded[:-2]) / 2.0

def grow_both(field):
    return pad_axis(pad_axis(field, 1, 2), 2, 2)

def grow_strike(field):
    return pad_axis(field, 1, 2)

def grow_dip(field):
    return pad_axis(field, 2, 2)

def lookup(classes, table):
    labels = jnp.arange(NCLASS, dtype=jnp.int32)[:, None, None]
    return lax.optimization_barrier(jnp.sum(jnp.where(classes[None] == labels, table[:, None, None], 0.0), axis=0))

def reference(pressure, strike_vel, dip_vel, bathy_class, bulk_table, buoy_table, gravity, sensor_amp, sensor_owner, sensor_cell, probe_kernel):
    bulk = lookup(bathy_class, bulk_table)
    buoy = lookup(bathy_class, buoy_table)
    sensor_index = jnp.arange(SENSORS, dtype=jnp.int32)
    strike_of = sensor_index // (S_DEV * N_DIP)
    row_index = strike_of * CX + sensor_cell // CY
    column_index = sensor_owner[:, 0] * CY + sensor_cell % CY
    inject = jnp.zeros((STEPS, NX, NY), pressure.dtype).at[:, row_index, column_index].add(sensor_amp)
    vertical = jnp.zeros_like(pressure)
    for step in range(STEPS):
        extended = grow_both(pressure)
        strike_vel = strike_vel - time_step * buoy * fourth_diff(extended[:, :, 2:-2], 1)
        dip_vel = dip_vel - time_step * buoy * fourth_diff(extended[:, 2:-2, :], 2)
        vertical = vertical - time_step * buoy * depth_diff(pressure)
        divergence = fourth_diff(grow_strike(strike_vel), 1) + fourth_diff(grow_dip(dip_vel), 2) + depth_diff(vertical)
        pressure = pressure - time_step * bulk * divergence + time_step * gravity[:, None, None] * vertical
        pressure = pressure.at[-1].add(inject[step])
    seafloor = pressure[-1]
    scale = 1.0 / math.sqrt(NX * NY)

    def accumulate(block, total):
        start = (block * CX).astype(jnp.int32)
        rows_now = lax.dynamic_slice_in_dim(seafloor, start, CX, 0)
        kernel_now = lax.dynamic_slice_in_dim(probe_kernel, start, CX, 1).astype(pressure.dtype)
        panel = (kernel_now * rows_now[None] * scale).reshape(PROBES, CX * NY)
        return total + jnp.dot(panel, panel.T, precision=lax.Precision.HIGHEST)
    gram = lax.fori_loop(jnp.int32(0), jnp.int32(N_STRIKE), accumulate, jnp.zeros((PROBES, PROBES), pressure.dtype))
    panel_factor = jnp.linalg.cholesky(gram).T
    return (pressure, panel_factor)
```

```python
import functools
import math

import jax
import jax.numpy as jnp
from jax import lax
from jax.experimental import pallas as pl
from jax.experimental.pallas import tpu as pltpu
from jax.sharding import PartitionSpec as P

STEPS = 4
PROBES = 96
NCLASS = 8
LEV = 64
CX = 64
CY = 128
OFF = 8
ROWS = CX + 2 * OFF
GROUPS = LEV // 16
BLOCKS = CX // 8
time_step = 0.2

F32 = jnp.float32
VMEM = pl.BlockSpec(memory_space=pltpu.VMEM)
SMEM = pl.BlockSpec(memory_space=pltpu.SMEM)
ANY = pl.BlockSpec(memory_space=pltpu.MemorySpace.HBM)


def rolled(x, shift):
    return pltpu.roll(x, shift % CY, 1)


def lanes(shape=(8, CY)):
    return lax.broadcasted_iota(jnp.int32, shape, 1)


def lane_diff(x):
    return 8.0 * (rolled(x, -1) - rolled(x, 1)) - (rolled(x, -2) - rolled(x, 2))


def row_diff(ref, level, row):
    def at(shift):
        return ref[level, row + shift : row + shift + 8, :]

    return 8.0 * (at(1) - at(-1)) - (at(2) - at(-2))


def edge_fix(diff):
    spot = lanes() & 7

    def const(*pairs):
        out = jnp.zeros((8, CY), F32)
        for where, value in pairs:
            out = jnp.where(spot == where, value, out)
        return out

    return (
        const((4, -8.0)) * rolled(diff, 1)
        + const((4, 1.0), (5, 1.0)) * rolled(diff, 2)
        + const((3, 8.0)) * rolled(diff, -1)
        + const((2, -1.0), (3, -1.0)) * rolled(diff, -2)
    )


def block(index):
    return slice(8 * index, 8 * index + 8)


def padded(index):
    return slice(OFF + 8 * index, OFF + 8 * index + 8)


def pack(src, src_level, dst, dst_base, src_off):
    group_of = lanes() >> 3

    def one(group, _):
        for b in range(BLOCKS):
            acc = jnp.zeros((8, CY), F32)
            for j in range(16):
                x = src[src_level + group * 16 + j, src_off + 8 * b : src_off + 8 * b + 8, :]
                acc = jnp.where(group_of == j, rolled(x, 8 * j + 4), acc)
            dst[dst_base + group, block(b), :] = acc
        return 0

    lax.fori_loop(0, GROUPS, one, 0)


def load_kernel(
    bulk_t, buoy_t, bathy, p_hbm, u_hbm, v_hbm, p, u, v, bo, bk, last, first, side, sems
):
    copies = [
        pltpu.make_async_copy(p_hbm, p.at[1 : LEV + 1, OFF : OFF + CX, :], sems.at[0]),
        pltpu.make_async_copy(v_hbm, v, sems.at[1]),
        pltpu.make_async_copy(u_hbm, u.at[:, OFF : OFF + CX, :], sems.at[2]),
    ]
    for copy in copies:
        copy.start()
    zero = jnp.zeros((8, CY), F32)
    for level in (0, LEV + 1):
        for b in range(ROWS // 8):
            p[level, block(b), :] = zero
    group_of = lanes() >> 3
    bo[0:8, :] = zero
    bo[ROWS - 8 : ROWS, :] = zero
    for b in range(BLOCKS):
        label = bathy[block(b), :]
        bulk = zero
        buoy = zero
        for c in range(NCLASS):
            bulk = jnp.where(label == c, bulk_t[c], bulk)
            buoy = jnp.where(label == c, buoy_t[c], buoy)
        buoy = buoy * (time_step / 12.0)
        bk[block(b), :] = bulk * (time_step / 12.0)
        bo[padded(b), :] = buoy
        acc = zero
        for j in range(16):
            acc = jnp.where(group_of == j, rolled(buoy, 8 * j + 4), acc)
        side[2 * GROUPS, block(b), :] = acc
    copies[0].wait()
    pack(p, 1, side, 0, OFF)

    def strip(level, _):
        first[level, :, :] = p[level + 1, OFF : OFF + 4, :]
        last[level, :, :] = p[level + 1, OFF + CX - 4 : OFF + CX, :]
        return 0

    lax.fori_loop(0, LEV, strip, 0, unroll=8)
    copies[1].wait()
    pack(v, 0, side, GROUPS, 0)
    copies[2].wait()

    def strip_u(pair, _):
        for half in range(2):
            here = slice(2 * half, 2 * half + 2)
            first[LEV + pair, here, :] = u[2 * pair + half, OFF : OFF + 2, :]
            last[LEV + pair, here, :] = u[2 * pair + half, OFF + CX - 2 : OFF + CX, :]
        return 0

    lax.fori_loop(0, LEV // 2, strip_u, 0, unroll=4)
    first[LEV + LEV // 2, 0:2, :] = bo[OFF : OFF + 2, :]
    last[LEV + LEV // 2, 0:2, :] = bo[OFF + CX - 2 : OFF + CX, :]
    first[LEV + LEV // 2, 2:4, :] = jnp.zeros((2, CY), F32)
    last[LEV + LEV // 2, 2:4, :] = jnp.zeros((2, CY), F32)


def inner_kernel(started, *refs):
    if started:
        p, bo, _, _, _, u, v, w = refs
    else:
        p, bo, _, _, u, v, w = refs
        for b in range(BLOCKS):
            w[0, block(b), :] = jnp.zeros((8, CY), F32)
            w[LEV + 1, block(b), :] = jnp.zeros((8, CY), F32)

    def one(level, _):
        for b in range(BLOCKS):
            coef = bo[padded(b), :]
            lift = (6.0 * coef) * (p[level + 2, padded(b), :] - p[level, padded(b), :])
            if started:
                w[level + 1, block(b), :] = w[level + 1, block(b), :] - lift
            else:
                w[level + 1, block(b), :] = -lift
            here = p[level + 1, padded(b), :]
            v[level, block(b), :] = v[level, block(b), :] - coef * lane_diff(here)
            if 0 < b < BLOCKS - 1:
                grad = row_diff(p, level + 1, OFF + 8 * b)
                u[level, padded(b), :] = u[level, padded(b), :] - coef * grad
        return 0

    lax.fori_loop(0, LEV, one, 0, unroll=2)


def sensor_kernel(table, sc, inj):
    me = sc[LEV + 4]
    lane = lanes((1, CY))
    for k in range(STEPS):
        for b in range(BLOCKS):
            inj[k, block(b), :] = jnp.zeros((8, CY), F32)

    def one(s, _):
        d, i = s // 8, s % 8
        keep = jnp.where(table[d, 32 + i] == me, 1.0, 0.0)
        cell = table[d, 40 + i].astype(jnp.int32)
        row, col = cell // CY, cell % CY
        hit = lane == col
        for k in range(STEPS):
            add = jnp.where(hit, table[d, 8 * k + i] * keep, 0.0)
            inj[k, pl.ds(row, 1), :] = inj[k, pl.ds(row, 1), :] + add
        return 0

    lax.fori_loop(0, 64, one, 0)


def outer_kernel(step, *refs):
    head, tail = step == 0, step == STEPS - 1
    refs = list(refs)
    take = lambda n: [refs.pop(0) for _ in range(n)]
    sc, bk, inj, w, own, from_up, from_down, from_left, from_right = take(9)
    _, _, _, _ = take(4)
    if not head:
        bo_a, bo_b = take(2)
        _, _ = take(2)
    p, u, v, bo = take(4)
    if head:
        bo_a, bo_b = take(2)
    va, vb = take(2)
    if tail:
        out, floor = take(2)
    else:
        last, first, side = take(3)
    fix_p, fix_v = take(2)
    if tail:
        (sems,) = take(1)

    low_half = (lanes() & 7) < 4
    keep_up, keep_down, keep_left, keep_right = (sc[LEV + i] for i in range(4))

    def halo(level, _):
        p[level + 1, OFF - 4 : OFF, :] = from_up[level, :, :] * keep_up
        p[level + 1, OFF + CX : OFF + CX + 4, :] = from_down[level, :, :] * keep_down
        return 0

    lax.fori_loop(0, LEV, halo, 0, unroll=8)

    if head:

        def halo_u(pair, _):
            for half in range(2):
                here = slice(2 * half, 2 * half + 2)
                level = 2 * pair + half
                u[level, OFF - 2 : OFF, :] = from_up[LEV + pair, here, :] * keep_up
                u[level, OFF + CX : OFF + CX + 2, :] = from_down[LEV + pair, here, :] * keep_down
            return 0

        lax.fori_loop(0, LEV // 2, halo_u, 0, unroll=4)
        bo[OFF - 2 : OFF, :] = from_up[LEV + LEV // 2, 0:2, :] * keep_up
        bo[OFF + CX : OFF + CX + 2, :] = from_down[LEV + LEV // 2, 0:2, :] * keep_down
        for b in range(BLOCKS):
            mine = own[2 * GROUPS, block(b), :]
            left = from_left[2 * GROUPS, block(b), :] * keep_left
            right = from_right[2 * GROUPS, block(b), :] * keep_right
            bo_a[block(b), :] = jnp.where(low_half, left, mine)
            bo_b[block(b), :] = jnp.where(low_half, mine, right)
            for g in range(GROUPS):
                mine = own[GROUPS + g, block(b), :]
                left = from_left[GROUPS + g, block(b), :] * keep_left
                right = from_right[GROUPS + g, block(b), :] * keep_right
                va[g, block(b), :] = jnp.where(low_half, left, mine)
                vb[g, block(b), :] = jnp.where(low_half, mine, right)

    def sides(g, _):
        for b in range(BLOCKS):
            mine = own[g, block(b), :]
            a = jnp.where(low_half, from_left[g, block(b), :] * keep_left, mine)
            c = jnp.where(low_half, mine, from_right[g, block(b), :] * keep_right)
            fix_p[g, block(b), :] = edge_fix(jnp.where(low_half, a - c, c - a))
            new_a = va[g, block(b), :] - bo_a[block(b), :] * lane_diff(a)
            new_b = vb[g, block(b), :] - bo_b[block(b), :] * lane_diff(c)
            va[g, block(b), :] = new_a
            vb[g, block(b), :] = new_b
            fix_v[g, block(b), :] = edge_fix(jnp.where(low_half, new_a - new_b, new_b - new_a))
        return 0

    lax.fori_loop(0, GROUPS, sides, 0)

    def rims(level, _):
        for row in (0, OFF, CX, CX + OFF):
            at = slice(row, row + 8)
            if row == 0:
                grad = row_diff(p, level + 1, 2)[0:8, :]
                u[level, 2:8, :] = u[level, 2:8, :] - bo[2:8, :] * grad[0:6, :]
            elif row == CX + OFF:
                grad = row_diff(p, level + 1, row - 2)
                u[level, row : row + 6, :] = (
                    u[level, row : row + 6, :] - bo[row : row + 6, :] * grad[2:8, :]
                )
            else:
                grad = row_diff(p, level + 1, row)
                u[level, at, :] = u[level, at, :] - bo[at, :] * grad
        return 0

    lax.fori_loop(0, LEV, rims, 0, unroll=2)

    for b in range(BLOCKS):
        p[LEV, padded(b), :] = p[LEV, padded(b), :] + inj[step, block(b), :]

    lane = lanes()
    edge = jnp.where((lane < 2) | (lane >= CY - 2), 1.0, 0.0)
    group_of = lane >> 3

    def one(level, _):
        group = level // 16
        j = level % 16
        back = CY - (8 * j + 4)
        lift = sc[level]
        mine = group_of == j
        for b in range(BLOCKS):
            coef = bo[padded(b), :] * edge
            new_v = v[level, block(b), :] - coef * pltpu.roll(fix_p[group, block(b), :], back, 1)
            v[level, block(b), :] = new_v
            div = lane_diff(new_v) + edge * pltpu.roll(fix_v[group, block(b), :], back, 1)
            div = div + row_diff(u, level, OFF + 8 * b)
            div = div + 6.0 * (w[level + 2, block(b), :] - w[level, block(b), :])
            new_p = p[level + 1, padded(b), :] - bk[block(b), :] * div
            new_p = new_p + lift * w[level + 1, block(b), :]
            p[level + 1, padded(b), :] = new_p
            if not tail:
                side[group, block(b), :] = jnp.where(
                    mine, pltpu.roll(new_p, 8 * j + 4, 1), side[group, block(b), :]
                )
        if not tail:
            first[level, :, :] = p[level + 1, OFF : OFF + 4, :]
            last[level, :, :] = p[level + 1, OFF + CX - 4 : OFF + CX, :]
        return 0

    if not tail:
        lax.fori_loop(0, LEV, one, 0, unroll=2)
    else:
        lax.fori_loop(0, LEV, one, 0, unroll=2)
        copy = pltpu.make_async_copy(
            p.at[1 : LEV + 1, OFF : OFF + CX, :], out, sems.at[0]
        )
        copy.start()
        floor[...] = p[LEV, OFF : OFF + CX, :]
        copy.wait()


def shaped(*shape):
    return jax.ShapeDtypeStruct(shape, F32)


def params(mib):
    return pltpu.CompilerParams(vmem_limit_bytes=mib << 20)


def cost(mib):
    return pl.CostEstimate(flops=20_000_000, bytes_accessed=mib << 20, transcendentals=0)


P_SHAPE = shaped(LEV + 2, ROWS, CY)
U_SHAPE = shaped(LEV, ROWS, CY)
V_SHAPE = shaped(LEV, CX, CY)
W_SHAPE = shaped(LEV + 2, CX, CY)
BO_SHAPE = shaped(ROWS, CY)
MAP = shaped(CX, CY)
SIDE = shaped(GROUPS, CX, CY)
STRIP = shaped(LEV, 4, CY)


def load(bulk_t, buoy_t, bathy, p, u, v):
    wide = shaped(LEV + LEV // 2 + 1, 4, CY)
    return pl.pallas_call(
        load_kernel,
        out_shape=(
            P_SHAPE, U_SHAPE, V_SHAPE, BO_SHAPE, MAP, wide, wide,
            shaped(2 * GROUPS + 1, CX, CY),
        ),
        in_specs=[SMEM, SMEM, VMEM, ANY, ANY, ANY],
        out_specs=[VMEM] * 8,
        scratch_shapes=[pltpu.SemaphoreType.DMA((3,))],
        compiler_params=params(16),
        name="load",
    )(bulk_t, buoy_t, bathy, p, u, v)


def inner(p, bo, u, v, w):
    started = w is not None
    args = (p, bo, u, v) + ((w,) if started else ())
    return pl.pallas_call(
        functools.partial(inner_kernel, started),
        out_shape=(U_SHAPE, V_SHAPE, W_SHAPE),
        in_specs=[VMEM] * len(args),
        out_specs=[VMEM] * 3,
        input_output_aliases={2: 0, 3: 1, 4: 2} if started else {2: 0, 3: 1},
        compiler_params=params(16),
        cost_estimate=cost(8),
        name="inner",
    )(*args)


def sensors(table, sc):
    return pl.pallas_call(
        sensor_kernel,
        out_shape=shaped(STEPS, CX, CY),
        in_specs=[SMEM, SMEM],
        out_specs=VMEM,
        compiler_params=params(4),
        name="sensors",
    )(table, sc)


def outer(step, sc, bk, inj, w, own, up, down, left, right, p, u, v, bo, state):
    head, tail = step == 0, step == STEPS - 1
    args = [sc, bk, inj, w, own, up, down, left, right, p, u, v, bo]
    shapes = [P_SHAPE, U_SHAPE, V_SHAPE, BO_SHAPE]
    alias = {9: 0, 10: 1, 11: 2, 12: 3}
    specs = [VMEM] * 4
    if head:
        shapes += [MAP, MAP, SIDE, SIDE]
        specs += [VMEM] * 4
    else:
        args += list(state)
        shapes += [SIDE, SIDE]
        specs += [VMEM] * 2
        alias.update({15: 4, 16: 5})
    scratch = [pltpu.VMEM((GROUPS, CX, CY), F32)] * 2
    if tail:
        shapes += [V_SHAPE, MAP]
        specs += [ANY, VMEM]
        scratch += [pltpu.SemaphoreType.DMA((1,))]
    else:
        shapes += [STRIP, STRIP, SIDE]
        specs += [VMEM] * 3
    return pl.pallas_call(
        functools.partial(outer_kernel, step),
        out_shape=tuple(shapes),
        in_specs=[SMEM] + [VMEM] * (len(args) - 1),
        out_specs=specs,
        scratch_shapes=scratch,
        input_output_aliases=alias,
        compiler_params=params(20),
        cost_estimate=cost(12),
        name="outer",
    )(*args)


def ring(x, axis, by):
    n = lax.axis_size(axis)
    return lax.ppermute(x, axis, [(i, (i + by) % n) for i in range(n)])


def swap(x, axis, bit):
    n = lax.axis_size(axis)
    return lax.ppermute(x, axis, [(i, i ^ bit) for i in range(n)])


def turned(x, axis, stride, by):
    n = lax.axis_size(axis)

    def to(i):
        digit = (i // stride) % 4
        return i + ((digit + by) % 4 - digit) * stride

    return lax.ppermute(x, axis, [(i, to(i)) for i in range(n)])


def total(x):
    x = x + swap(x, "dip", 1)
    for axis, stride in (("dip", 2), ("strike", 1), ("strike", 4)):
        x = x + turned(x, axis, stride, 1) + turned(x, axis, stride, 2) + turned(x, axis, stride, 3)
    return x


def body(
    pressure,
    strike_vel,
    dip_vel,
    bathy_class,
    bulk_table,
    buoy_table,
    gravity,
    sensor_amp,
    sensor_owner,
    sensor_cell,
    probe_kernel,
):
    strike, dip = lax.axis_index("strike"), lax.axis_index("dip")
    strikes, dips = lax.axis_size("strike"), lax.axis_size("dip")
    flags = jnp.stack(
        [strike > 0, strike < strikes - 1, dip > 0, dip < dips - 1]
    ).astype(F32)
    sc = jnp.concatenate(
        [time_step * gravity, flags, dip.astype(F32)[None], jnp.zeros((59,), F32)]
    )
    table = jnp.concatenate(
        [
            sensor_amp.reshape(-1),
            sensor_owner[:, 0].astype(F32),
            sensor_cell.astype(F32),
            jnp.zeros((16,), F32),
        ]
    )
    slots = jnp.arange(dips, dtype=jnp.int32)[:, None]
    table = jnp.where(slots == dip, table[None], 0.0)
    table, sc, pressure = lax.optimization_barrier((table, sc, pressure))
    for bit in (1, 2, 4):
        table = table + swap(table, "dip", bit)
    inj = sensors(table, sc)

    p, u, v, bo, bk, last, first, side = load(
        bulk_table, buoy_table, bathy_class, pressure, strike_vel, dip_vel
    )
    w = None
    state = None
    for step in range(STEPS):
        up, down = ring(last, "strike", 1), ring(first, "strike", -1)
        left, right = ring(side, "dip", 1), ring(side, "dip", -1)
        u, v, w = inner(p, bo, u, v, w)
        res = outer(step, sc, bk, inj, w, side, up, down, left, right, p, u, v, bo, state)
        p, u, v, bo = res[:4]
        if step == 0:
            state = res[4:8]
            rest = res[8:]
        else:
            state = state[:2] + res[4:6]
            rest = res[6:]
        if step < STEPS - 1:
            last, first, side = rest
        else:
            final, seafloor = rest
    cells = CX * CY
    total_cells = cells * strikes * dips
    scale = 1.0 / math.sqrt(total_cells)
    panel = (probe_kernel.astype(F32) * seafloor[None] * scale).reshape(PROBES, cells)
    gram = jnp.dot(panel, panel.T, precision=lax.Precision.HIGHEST)
    gram = total(gram)
    return (final, jnp.linalg.cholesky(gram).T)


def solution(mesh):
    return jax.shard_map(
        body,
        mesh=mesh,
        in_specs=(
            P(None, "strike", "dip"),
            P(None, "strike", "dip"),
            P(None, "strike", "dip"),
            P("strike", "dip"),
            P(),
            P(),
            P(),
            P(None, ("strike", "dip")),
            P(("strike", "dip"), None),
            P(("strike", "dip")),
            P(None, "strike", "dip"),
        ),
        out_specs=(P(None, "strike", "dip"), P()),
        check_vma=False,
    )
```

```python
import functools
import math

import jax
import jax.numpy as jnp
from jax import lax
from jax.experimental import pallas as pl
from jax.experimental.pallas import tpu as pltpu
from jax.sharding import PartitionSpec as P

STEPS = 4
PROBES = 96
NCLASS = 8
LEV = 64
CX = 64
CY = 128
OFF = 8
ROWS = CX + 2 * OFF
GROUPS = LEV // 16
BLOCKS = CX // 8
BATCH = 4
time_step = 0.2

F32 = jnp.float32
VMEM = pl.BlockSpec(memory_space=pltpu.VMEM)
SMEM = pl.BlockSpec(memory_space=pltpu.SMEM)
ANY = pl.BlockSpec(memory_space=pltpu.MemorySpace.HBM)


def rolled(x, shift):
    return pltpu.roll(x, shift % CY, 1)


def lanes(shape=(8, CY)):
    return lax.broadcasted_iota(jnp.int32, shape, 1)


def lane_diff(x):
    return 8.0 * (rolled(x, -1) - rolled(x, 1)) - (rolled(x, -2) - rolled(x, 2))


def row_diff(ref, level, row):
    def at(shift):
        return ref[level, row + shift : row + shift + 8, :]

    return 8.0 * (at(1) - at(-1)) - (at(2) - at(-2))


def fill_taps(taps):
    shape = (2 * CY, CY)
    source = lax.broadcasted_iota(jnp.int32, shape, 0) & (CY - 1)
    ahead = (source - lax.broadcasted_iota(jnp.int32, shape, 1)) & (CY - 1)
    value = jnp.where(ahead == 1, 8.0, 0.0) - jnp.where(ahead == CY - 1, 8.0, 0.0)
    value = value - jnp.where(ahead == 2, 1.0, 0.0) + jnp.where(ahead == CY - 2, 1.0, 0.0)
    taps[...] = value.astype(jnp.bfloat16)


def lane_diff(x, taps):
    high = x.astype(jnp.bfloat16)
    low = (x - high.astype(F32)).astype(jnp.bfloat16)
    parts = jnp.concatenate([high, low], axis=1)
    return jnp.dot(parts, taps[...], preferred_element_type=F32)


def block(index):
    return slice(8 * index, 8 * index + 8)


def padded(index):
    return slice(OFF + 8 * index, OFF + 8 * index + 8)


def pack(src, src_level, dst, dst_base, src_off):
    group_of = lanes() >> 3

    def one(group, _):
        for b in range(BLOCKS):
            acc = jnp.zeros((8, CY), F32)
            for j in range(16):
                x = src[src_level + group * 16 + j, src_off + 8 * b : src_off + 8 * b + 8, :]
                acc = jnp.where(group_of == j, rolled(x, 8 * j + 4), acc)
            dst[dst_base + group, block(b), :] = acc
        return 0

    lax.fori_loop(0, GROUPS, one, 0)


def prep_kernel(gravity_h, amp_h, owner_h, cell_h, sc, table, gravity, amp, owner, cell, sems):
    pairs = ((gravity_h, gravity), (amp_h, amp), (owner_h, owner), (cell_h, cell))
    copies = [pltpu.make_async_copy(a, b, sems.at[i]) for i, (a, b) in enumerate(pairs)]
    for copy in copies:
        copy.start()
    strike, dip = lax.axis_index("strike"), lax.axis_index("dip")
    lane, row = lanes((8, CY)), lax.broadcasted_iota(jnp.int32, (8, CY), 0)
    flags = [
        strike > 0,
        strike < lax.axis_size("strike") - 1,
        dip > 0,
        dip < lax.axis_size("dip") - 1,
    ]
    scalars = jnp.zeros((8, CY), F32)
    for i, flag in enumerate(flags):
        scalars = jnp.where(lane == LEV + i, jnp.where(flag, 1.0, 0.0), scalars)
    scalars = jnp.where(lane == LEV + 4, dip.astype(F32), scalars)
    for copy in copies:
        copy.wait()
    for level in range(LEV):
        scalars = jnp.where(lane == level, time_step * gravity[level], scalars)
    sc[...] = scalars
    sheet = jnp.zeros((8, CY), F32)
    for i in range(8):
        for k in range(STEPS):
            sheet = jnp.where(lane == 8 * k + i, amp[k, i], sheet)
        sheet = jnp.where(lane == 32 + i, owner[i].astype(F32), sheet)
        sheet = jnp.where(lane == 40 + i, (cell[i] // CY).astype(F32), sheet)
        sheet = jnp.where(lane == 48 + i, (cell[i] % CY).astype(F32), sheet)
    table[...] = jnp.where(row == dip, sheet, 0.0)


def load_kernel(
    bulk_h, buoy_h, bathy_h, p_hbm, u_hbm, v_hbm, p, u, v, bo, bk, last, first, side,
    bulk_t, buoy_t, bathy, sems
):
    small = [
        pltpu.make_async_copy(bathy_h, bathy, sems.at[3]),
        pltpu.make_async_copy(bulk_h, bulk_t, sems.at[4]),
        pltpu.make_async_copy(buoy_h, buoy_t, sems.at[5]),
    ]
    for copy in small:
        copy.start()
    copies = [
        pltpu.make_async_copy(p_hbm, p.at[1 : LEV + 1, OFF : OFF + CX, :], sems.at[0]),
        pltpu.make_async_copy(v_hbm, v, sems.at[1]),
        pltpu.make_async_copy(u_hbm, u.at[:, OFF : OFF + CX, :], sems.at[2]),
    ]
    for copy in copies:
        copy.start()
    zero = jnp.zeros((8, CY), F32)
    for level in (0, LEV + 1):
        for b in range(ROWS // 8):
            p[level, block(b), :] = zero
    group_of = lanes() >> 3
    for copy in small:
        copy.wait()
    bo[0:8, :] = zero
    bo[ROWS - 8 : ROWS, :] = zero
    for b in range(BLOCKS):
        label = bathy[block(b), :]
        bulk = zero
        buoy = zero
        for c in range(NCLASS):
            bulk = jnp.where(label == c, bulk_t[c], bulk)
            buoy = jnp.where(label == c, buoy_t[c], buoy)
        buoy = buoy * (time_step / 12.0)
        bk[block(b), :] = bulk * (time_step / 12.0)
        bo[padded(b), :] = buoy
        acc = zero
        for j in range(16):
            acc = jnp.where(group_of == j, rolled(buoy, 8 * j + 4), acc)
        side[2 * GROUPS, block(b), :] = acc
    copies[0].wait()
    pack(p, 1, side, 0, OFF)

    def strip(level, _):
        first[level, :, :] = p[level + 1, OFF : OFF + 4, :]
        last[level, :, :] = p[level + 1, OFF + CX - 4 : OFF + CX, :]
        return 0

    lax.fori_loop(0, LEV, strip, 0, unroll=8)
    copies[1].wait()
    pack(v, 0, side, GROUPS, 0)
    copies[2].wait()

    def strip_u(pair, _):
        for half in range(2):
            here = slice(2 * half, 2 * half + 2)
            first[LEV + pair, here, :] = u[2 * pair + half, OFF : OFF + 2, :]
            last[LEV + pair, here, :] = u[2 * pair + half, OFF + CX - 2 : OFF + CX, :]
        return 0

    lax.fori_loop(0, LEV // 2, strip_u, 0, unroll=4)
    first[LEV + LEV // 2, 0:2, :] = bo[OFF : OFF + 2, :]
    last[LEV + LEV // 2, 0:2, :] = bo[OFF + CX - 2 : OFF + CX, :]
    first[LEV + LEV // 2, 2:4, :] = jnp.zeros((2, CY), F32)
    last[LEV + LEV // 2, 2:4, :] = jnp.zeros((2, CY), F32)


def inner_kernel(started, *refs):
    if started:
        p, bo, _, _, _, u, v, w, taps = refs
    else:
        p, bo, _, _, u, v, w, taps = refs
        for b in range(BLOCKS):
            w[0, block(b), :] = jnp.zeros((8, CY), F32)
            w[LEV + 1, block(b), :] = jnp.zeros((8, CY), F32)
    fill_taps(taps)

    def batch(index, _):
        base = index * BATCH
        field = p[pl.ds(base + 1, BATCH), OFF : OFF + CX, :].reshape(BATCH * CX, CY)
        slope = lane_diff(field, taps)
        for i in range(BATCH):
            level = base + i
            for b in range(BLOCKS):
                coef = bo[padded(b), :]
                part = slope[i * CX + 8 * b : i * CX + 8 * b + 8, :]
                v[level, block(b), :] = v[level, block(b), :] - coef * part
                lift = (6.0 * coef) * (p[level + 2, padded(b), :] - p[level, padded(b), :])
                if started:
                    w[level + 1, block(b), :] = w[level + 1, block(b), :] - lift
                else:
                    w[level + 1, block(b), :] = -lift
                if 0 < b < BLOCKS - 1:
                    grad = row_diff(p, level + 1, OFF + 8 * b)
                    u[level, padded(b), :] = u[level, padded(b), :] - coef * grad
        return 0

    lax.fori_loop(0, LEV // BATCH, batch, 0)


def sensor_kernel(table, sc, inj):
    me = sc[0, LEV + 4]
    lane = lanes((1, CY))
    for k in range(STEPS):
        for b in range(BLOCKS):
            inj[k, block(b), :] = jnp.zeros((8, CY), F32)

    def one(d, _):
        for i in range(8):
            keep = jnp.where(table[d, 32 + i] == me, 1.0, 0.0)
            row = table[d, 40 + i].astype(jnp.int32)
            hit = lane == table[d, 48 + i].astype(jnp.int32)
            for k in range(STEPS):
                add = jnp.where(hit, table[d, 8 * k + i] * keep, 0.0)
                inj[k, pl.ds(row, 1), :] = inj[k, pl.ds(row, 1), :] + add
        return 0

    lax.fori_loop(0, 8, one, 0)


def outer_kernel(step, *refs):
    head, tail = step == 0, step == STEPS - 1
    refs = list(refs)
    take = lambda n: [refs.pop(0) for _ in range(n)]
    sc, bk, inj, w, v, own, from_up, from_down, from_left, from_right = take(10)
    _, _, _ = take(3)
    if not head:
        bo_a, bo_b, bo_c = take(3)
        _, _, _ = take(3)
    p, u, bo = take(3)
    if head:
        bo_a, bo_b, bo_c = take(3)
    va, vb, vc = take(3)
    if tail:
        out, floor = take(2)
    else:
        last, first, side = take(3)
    fix, taps = take(2)
    if tail:
        (sems,) = take(1)
    fill_taps(taps)

    keep_up, keep_down, keep_left, keep_right = (sc[0, LEV + i] for i in range(4))

    def halo(level, _):
        p[level + 1, OFF - 4 : OFF, :] = from_up[level, :, :] * keep_up
        p[level + 1, OFF + CX : OFF + CX + 4, :] = from_down[level, :, :] * keep_down
        return 0

    lax.fori_loop(0, LEV, halo, 0, unroll=8)

    spot = lanes((CX, CY)) & 7
    low_half = spot < 4
    if head:

        def halo_u(pair, _):
            for half in range(2):
                here = slice(2 * half, 2 * half + 2)
                level = 2 * pair + half
                u[level, OFF - 2 : OFF, :] = from_up[LEV + pair, here, :] * keep_up
                u[level, OFF + CX : OFF + CX + 2, :] = from_down[LEV + pair, here, :] * keep_down
            return 0

        lax.fori_loop(0, LEV // 2, halo_u, 0, unroll=4)
        bo[OFF - 2 : OFF, :] = from_up[LEV + LEV // 2, 0:2, :] * keep_up
        bo[OFF + CX : OFF + CX + 2, :] = from_down[LEV + LEV // 2, 0:2, :] * keep_down
        mine = own[2 * GROUPS]
        bo_a[...] = jnp.where(low_half, from_left[2 * GROUPS] * keep_left, mine)
        bo_b[...] = jnp.where(low_half, mine, from_right[2 * GROUPS] * keep_right)
        bo_c[...] = mine
        for g in range(GROUPS):
            mine = own[GROUPS + g]
            va[g] = jnp.where(low_half, from_left[GROUPS + g] * keep_left, mine)
            vb[g] = jnp.where(low_half, mine, from_right[GROUPS + g] * keep_right)
            vc[g] = mine

    def sides(g, _):
        middle = (spot >= 2) & (spot < 6)
        mine = own[g]
        a = jnp.where(low_half, from_left[g] * keep_left, mine)
        c = jnp.where(low_half, mine, from_right[g] * keep_right)
        slope = lane_diff(jnp.concatenate([a, c, mine], axis=0), taps)
        new_a = va[g] - bo_a[...] * slope[0:CX]
        new_b = vb[g] - bo_b[...] * slope[CX : 2 * CX]
        new_c = vc[g] - bo_c[...] * slope[2 * CX : 3 * CX]
        va[g] = new_a
        vb[g] = new_b
        vc[g] = new_c
        rest = jnp.concatenate(
            [
                jnp.where(middle, new_a - new_c, 0.0),
                jnp.where(middle, new_b - new_c, 0.0),
            ],
            axis=0,
        )
        slope = lane_diff(rest, taps)
        fix[g] = jnp.where(low_half, slope[CX : 2 * CX], slope[0:CX])
        return 0

    lax.fori_loop(0, GROUPS, sides, 0)

    def rims(level, _):
        for row in (0, OFF, CX, CX + OFF):
            at = slice(row, row + 8)
            if row == 0:
                grad = row_diff(p, level + 1, 2)[0:8, :]
                u[level, 2:8, :] = u[level, 2:8, :] - bo[2:8, :] * grad[0:6, :]
            elif row == CX + OFF:
                grad = row_diff(p, level + 1, row - 2)
                u[level, row : row + 6, :] = (
                    u[level, row : row + 6, :] - bo[row : row + 6, :] * grad[2:8, :]
                )
            else:
                grad = row_diff(p, level + 1, row)
                u[level, at, :] = u[level, at, :] - bo[at, :] * grad
        return 0

    lax.fori_loop(0, LEV, rims, 0, unroll=8)

    for b in range(BLOCKS):
        p[LEV, padded(b), :] = p[LEV, padded(b), :] + inj[step, block(b), :]

    lane = lanes()
    edge = jnp.where((lane < 4) | (lane >= CY - 4), 1.0, 0.0)
    group_of = lane >> 3

    def one(group, _):
        packed = [jnp.zeros((8, CY), F32)] * BLOCKS
        for q in range(16 // BATCH):
            base = group * 16 + q * BATCH
            slope = lane_diff(v[pl.ds(base, BATCH)].reshape(BATCH * CX, CY), taps)
            for i in range(BATCH):
                level = base + i
                j = q * BATCH + i
                lift = sc[0, level]
                for b in range(BLOCKS):
                    div = slope[i * CX + 8 * b : i * CX + 8 * b + 8, :]
                    div = div + edge * rolled(fix[group, block(b), :], -(8 * j + 4))
                    div = div + row_diff(u, level, OFF + 8 * b)
                    div = div + 6.0 * (w[level + 2, block(b), :] - w[level, block(b), :])
                    new_p = p[level + 1, padded(b), :] - bk[block(b), :] * div
                    new_p = new_p + lift * w[level + 1, block(b), :]
                    p[level + 1, padded(b), :] = new_p
                    if not tail:
                        packed[b] = jnp.where(group_of == j, rolled(new_p, 8 * j + 4), packed[b])
                        if b == 0:
                            first[level, :, :] = new_p[0:4, :]
                        if b == BLOCKS - 1:
                            last[level, :, :] = new_p[4:8, :]
        if not tail:
            for b in range(BLOCKS):
                side[group, block(b), :] = packed[b]
        return 0

    lax.fori_loop(0, GROUPS, one, 0)
    if tail:
        copy = pltpu.make_async_copy(
            p.at[1 : LEV + 1, OFF : OFF + CX, :], out, sems.at[0]
        )
        copy.start()
        floor[...] = p[LEV, OFF : OFF + CX, :]
        copy.wait()


def kept(*arrays):
    space = pltpu.MemorySpace.HBM
    return [pltpu.with_memory_space_constraint(x, space) for x in arrays]


def shaped(*shape):
    return jax.ShapeDtypeStruct(shape, F32)


def params(mib):
    return pltpu.CompilerParams(vmem_limit_bytes=mib << 20)


def cost(mib):
    return pl.CostEstimate(flops=20_000_000, bytes_accessed=mib << 20, transcendentals=0)


P_SHAPE = shaped(LEV + 2, ROWS, CY)
U_SHAPE = shaped(LEV, ROWS, CY)
V_SHAPE = shaped(LEV, CX, CY)
W_SHAPE = shaped(LEV + 2, CX, CY)
BO_SHAPE = shaped(ROWS, CY)
MAP = shaped(CX, CY)
TAPS = pltpu.VMEM((2 * CY, CY), jnp.bfloat16)
SIDE = shaped(GROUPS, CX, CY)
STRIP = shaped(LEV, 4, CY)


def prep(gravity, amp, owner, cell):
    return pl.pallas_call(
        prep_kernel,
        out_shape=(shaped(8, CY), shaped(8, CY)),
        in_specs=[ANY] * 4,
        out_specs=[VMEM] * 2,
        scratch_shapes=[
            pltpu.SMEM((LEV,), F32),
            pltpu.SMEM((STEPS, 8), F32),
            pltpu.SMEM((8,), jnp.int32),
            pltpu.SMEM((8,), jnp.int32),
            pltpu.SemaphoreType.DMA((4,)),
        ],
        compiler_params=params(4),
        name="prep",
    )(*kept(gravity, amp, owner, cell))


def load(bulk_t, buoy_t, bathy, p, u, v):
    wide = shaped(LEV + LEV // 2 + 1, 4, CY)
    return pl.pallas_call(
        load_kernel,
        out_shape=(
            P_SHAPE, U_SHAPE, V_SHAPE, BO_SHAPE, MAP, wide, wide,
            shaped(2 * GROUPS + 1, CX, CY),
        ),
        in_specs=[ANY] * 6,
        out_specs=[VMEM] * 8,
        scratch_shapes=[
            pltpu.SMEM((NCLASS,), F32),
            pltpu.SMEM((NCLASS,), F32),
            pltpu.VMEM((CX, CY), jnp.int32),
            pltpu.SemaphoreType.DMA((6,)),
        ],
        compiler_params=params(16),
        cost_estimate=cost(8),
        name="load",
    )(*kept(bulk_t, buoy_t, bathy, p, u, v))


def inner(p, bo, u, v, w):
    started = w is not None
    args = (p, bo, u, v) + ((w,) if started else ())
    return pl.pallas_call(
        functools.partial(inner_kernel, started),
        out_shape=(U_SHAPE, V_SHAPE, W_SHAPE),
        in_specs=[VMEM] * len(args),
        out_specs=[VMEM] * 3,
        scratch_shapes=[TAPS],
        input_output_aliases={2: 0, 3: 1, 4: 2} if started else {2: 0, 3: 1},
        compiler_params=params(16),
        cost_estimate=cost(8),
        name="inner",
    )(*args)


def sensors(table, sc):
    return pl.pallas_call(
        sensor_kernel,
        out_shape=shaped(STEPS, CX, CY),
        in_specs=[SMEM, SMEM],
        out_specs=VMEM,
        compiler_params=params(4),
        name="sensors",
    )(table, sc)


def outer(step, sc, bk, inj, w, v, own, up, down, left, right, p, u, bo, state):
    head, tail = step == 0, step == STEPS - 1
    args = [sc, bk, inj, w, v, own, up, down, left, right, p, u, bo]
    shapes = [P_SHAPE, U_SHAPE, BO_SHAPE]
    alias = {10: 0, 11: 1, 12: 2}
    specs = [VMEM] * 3
    if head:
        shapes += [MAP, MAP, MAP, SIDE, SIDE, SIDE]
        specs += [VMEM] * 6
    else:
        args += list(state)
        shapes += [SIDE, SIDE, SIDE]
        specs += [VMEM] * 3
        alias.update({16: 3, 17: 4, 18: 5})
    scratch = [pltpu.VMEM((GROUPS, CX, CY), F32), TAPS]
    if tail:
        shapes += [V_SHAPE, MAP]
        specs += [ANY, VMEM]
        scratch += [pltpu.SemaphoreType.DMA((1,))]
    else:
        shapes += [STRIP, STRIP, SIDE]
        specs += [VMEM] * 3
    return pl.pallas_call(
        functools.partial(outer_kernel, step),
        out_shape=tuple(shapes),
        in_specs=[SMEM] + [VMEM] * (len(args) - 1),
        out_specs=specs,
        scratch_shapes=scratch,
        input_output_aliases=alias,
        compiler_params=params(20),
        cost_estimate=cost(12),
        name="outer",
    )(*args)


def ring(x, axis, by):
    n = lax.axis_size(axis)
    return lax.ppermute(x, axis, [(i, (i + by) % n) for i in range(n)])


def swap(x, axis, bit):
    n = lax.axis_size(axis)
    return lax.ppermute(x, axis, [(i, i ^ bit) for i in range(n)])


def total(x):
    x = x + swap(x, "dip", 1)
    for axis, stride in (("dip", 2), ("strike", 1), ("strike", 4)):
        x = x + sum(swap(x, axis, stride * bits) for bits in (1, 2, 3))
    return x


def body(
    pressure,
    strike_vel,
    dip_vel,
    bathy_class,
    bulk_table,
    buoy_table,
    gravity,
    sensor_amp,
    sensor_owner,
    sensor_cell,
    probe_kernel,
):
    strikes, dips = lax.axis_size("strike"), lax.axis_size("dip")
    sc, table = prep(gravity, sensor_amp, sensor_owner[:, 0], sensor_cell)
    for bit in (1, 2, 4):
        table = table + swap(table, "dip", bit)
    inj = sensors(table, sc)

    p, u, v, bo, bk, last, first, side = load(
        bulk_table, buoy_table, bathy_class, pressure, strike_vel, dip_vel
    )
    w = None
    state = None
    for step in range(STEPS):
        up, down = ring(last, "strike", 1), ring(first, "strike", -1)
        left, right = ring(side, "dip", 1), ring(side, "dip", -1)
        u, v, w = inner(p, bo, u, v, w)
        res = outer(step, sc, bk, inj, w, v, side, up, down, left, right, p, u, bo, state)
        p, u, bo = res[:3]
        if step == 0:
            state = res[3:9]
            rest = res[9:]
        else:
            state = state[:3] + res[3:6]
            rest = res[6:]
        if step < STEPS - 1:
            last, first, side = rest
        else:
            final, seafloor = rest
    cells = CX * CY
    total_cells = cells * strikes * dips
    scale = 1.0 / math.sqrt(total_cells)
    panel = (probe_kernel.astype(F32) * seafloor[None] * scale).reshape(PROBES, cells)
    gram = jnp.dot(panel, panel.T, precision=lax.Precision.HIGHEST)
    gram = total(gram)
    return (final, jnp.linalg.cholesky(gram).T)


def solution(mesh):
    return jax.shard_map(
        body,
        mesh=mesh,
        in_specs=(
            P(None, "strike", "dip"),
            P(None, "strike", "dip"),
            P(None, "strike", "dip"),
            P("strike", "dip"),
            P(),
            P(),
            P(),
            P(None, ("strike", "dip")),
            P(("strike", "dip"), None),
            P(("strike", "dip")),
            P(None, "strike", "dip"),
        ),
        out_specs=(P(None, "strike", "dip"), P()),
        check_vma=False,
    )
```

```python
import functools
import math

import jax
import jax.numpy as jnp
from jax import lax
from jax.experimental import pallas as pl
from jax.experimental.pallas import tpu as pltpu
from jax.sharding import PartitionSpec as P

STEPS = 4
PROBES = 96
NCLASS = 8
LEV = 64
CX = 64
CY = 128
OFF = 8
ROWS = CX + 2 * OFF
GROUPS = LEV // 16
BLOCKS = CX // 8
BATCH = 16
time_step = 0.2

F32 = jnp.float32
VMEM = pl.BlockSpec(memory_space=pltpu.VMEM)
SMEM = pl.BlockSpec(memory_space=pltpu.SMEM)
ANY = pl.BlockSpec(memory_space=pltpu.MemorySpace.HBM)


def rolled(x, shift):
    return pltpu.roll(x, shift % CY, 1)


def lanes(shape=(8, CY)):
    return lax.broadcasted_iota(jnp.int32, shape, 1)


def lane_diff(x):
    return 8.0 * (rolled(x, -1) - rolled(x, 1)) - (rolled(x, -2) - rolled(x, 2))


def row_diff(ref, level, row):
    def at(shift):
        return ref[level, row + shift : row + shift + 8, :]

    return 8.0 * (at(1) - at(-1)) - (at(2) - at(-2))


def fill_taps(taps):
    shape = (2 * CY, CY)
    source = lax.broadcasted_iota(jnp.int32, shape, 0) & (CY - 1)
    ahead = (source - lax.broadcasted_iota(jnp.int32, shape, 1)) & (CY - 1)
    value = jnp.where(ahead == 1, 8.0, 0.0) - jnp.where(ahead == CY - 1, 8.0, 0.0)
    value = value - jnp.where(ahead == 2, 1.0, 0.0) + jnp.where(ahead == CY - 2, 1.0, 0.0)
    taps[...] = value.astype(jnp.bfloat16)


def lane_diff(x, taps):
    high = x.astype(jnp.bfloat16)
    low = (x - high.astype(F32)).astype(jnp.bfloat16)
    parts = jnp.concatenate([high, low], axis=1)
    return jnp.dot(parts, taps[...], preferred_element_type=F32)


def block(index):
    return slice(8 * index, 8 * index + 8)


def padded(index):
    return slice(OFF + 8 * index, OFF + 8 * index + 8)


def pack(src, src_level, dst, dst_base, src_off):
    group_of = lanes() >> 3

    def one(group, _):
        for b in range(BLOCKS):
            acc = jnp.zeros((8, CY), F32)
            for j in range(16):
                x = src[src_level + group * 16 + j, src_off + 8 * b : src_off + 8 * b + 8, :]
                acc = jnp.where(group_of == j, rolled(x, 8 * j + 4), acc)
            dst[dst_base + group, block(b), :] = acc
        return 0

    lax.fori_loop(0, GROUPS, one, 0)


def prep_kernel(gravity_h, amp_h, owner_h, cell_h, sc, table, gravity, amp, owner, cell, sems):
    pairs = ((gravity_h, gravity), (amp_h, amp), (owner_h, owner), (cell_h, cell))
    copies = [pltpu.make_async_copy(a, b, sems.at[i]) for i, (a, b) in enumerate(pairs)]
    for copy in copies:
        copy.start()
    dip = lax.axis_index("dip")
    lane, row = lanes((8, CY)), lax.broadcasted_iota(jnp.int32, (8, CY), 0)
    for copy in copies:
        copy.wait()
    for start in range(0, LEV, 8):
        part = jnp.zeros((8, CY), F32)
        for i in range(8):
            part = jnp.where(row == i, time_step / 6.0 * gravity[start + i], part)
        sc[start : start + 8, :] = part
    sheet = jnp.zeros((8, CY), F32)
    for i in range(8):
        for k in range(STEPS):
            sheet = jnp.where(lane == 8 * k + i, amp[k, i], sheet)
        sheet = jnp.where(lane == 32 + i, owner[i].astype(F32), sheet)
        sheet = jnp.where(lane == 40 + i, (cell[i] // CY).astype(F32), sheet)
        sheet = jnp.where(lane == 48 + i, (cell[i] % CY).astype(F32), sheet)
    table[...] = jnp.where(row == dip, sheet, 0.0)


def load_kernel(
    bulk_h, buoy_h, bathy_h, p_hbm, u_hbm, v_hbm, p, u, v, bo, bk, last, first, side,
    bulk_t, buoy_t, bathy, sems
):
    small = [
        pltpu.make_async_copy(bathy_h, bathy, sems.at[3]),
        pltpu.make_async_copy(bulk_h, bulk_t, sems.at[4]),
        pltpu.make_async_copy(buoy_h, buoy_t, sems.at[5]),
    ]
    for copy in small:
        copy.start()
    copies = [
        pltpu.make_async_copy(p_hbm, p.at[1 : LEV + 1, OFF : OFF + CX, :], sems.at[0]),
        pltpu.make_async_copy(v_hbm, v, sems.at[1]),
        pltpu.make_async_copy(u_hbm, u.at[:, OFF : OFF + CX, :], sems.at[2]),
    ]
    for copy in copies:
        copy.start()
    zero = jnp.zeros((8, CY), F32)
    for level in (0, LEV + 1):
        for b in range(ROWS // 8):
            p[level, block(b), :] = zero
    group_of = lanes() >> 3
    for copy in small:
        copy.wait()
    bo[0:8, :] = zero
    bo[ROWS - 8 : ROWS, :] = zero
    for b in range(BLOCKS):
        label = bathy[block(b), :]
        bulk = zero
        buoy = zero
        for c in range(NCLASS):
            bulk = jnp.where(label == c, bulk_t[c], bulk)
            buoy = jnp.where(label == c, buoy_t[c], buoy)
        buoy = buoy * (time_step / 12.0)
        bk[block(b), :] = bulk * (time_step / 12.0)
        bo[padded(b), :] = buoy
        acc = zero
        for j in range(16):
            acc = jnp.where(group_of == j, rolled(buoy, 8 * j + 4), acc)
        side[2 * GROUPS, block(b), :] = acc
    copies[0].wait()
    pack(p, 1, side, 0, OFF)

    def strip(level, _):
        first[level, :, :] = p[level + 1, OFF : OFF + 4, :]
        last[level, :, :] = p[level + 1, OFF + CX - 4 : OFF + CX, :]
        return 0

    lax.fori_loop(0, LEV, strip, 0, unroll=8)
    copies[1].wait()
    pack(v, 0, side, GROUPS, 0)
    copies[2].wait()

    def strip_u(pair, _):
        for half in range(2):
            here = slice(2 * half, 2 * half + 2)
            first[LEV + pair, here, :] = u[2 * pair + half, OFF : OFF + 2, :]
            last[LEV + pair, here, :] = u[2 * pair + half, OFF + CX - 2 : OFF + CX, :]
        return 0

    lax.fori_loop(0, LEV // 2, strip_u, 0, unroll=4)
    first[LEV + LEV // 2, 0:2, :] = bo[OFF : OFF + 2, :]
    last[LEV + LEV // 2, 0:2, :] = bo[OFF + CX - 2 : OFF + CX, :]
    first[LEV + LEV // 2, 2:4, :] = jnp.zeros((2, CY), F32)
    last[LEV + LEV // 2, 2:4, :] = jnp.zeros((2, CY), F32)


def inner_kernel(started, *refs):
    sc, bk, bo = refs[:3]
    p, u, v, w, rest, taps = refs[-6:]
    if not started:
        for b in range(BLOCKS):
            w[0, block(b), :] = jnp.zeros((8, CY), F32)
            w[LEV + 1, block(b), :] = jnp.zeros((8, CY), F32)
    fill_taps(taps)

    def motion(index, _):
        base = index * BATCH
        field = p[pl.ds(base + 1, BATCH), OFF : OFF + CX, :].reshape(BATCH * CX, CY)
        slope = lane_diff(field, taps)
        for b in range(BLOCKS):
            coef = bo[padded(b), :]
            lines = [p[base + i, padded(b), :] for i in range(BATCH + 2)]
            for i in range(BATCH):
                level = base + i
                part = slope[i * CX + 8 * b : i * CX + 8 * b + 8, :]
                v[level, block(b), :] = v[level, block(b), :] - coef * part
                lift = (36.0 * coef) * (lines[i + 2] - lines[i])
                if started:
                    w[level + 1, block(b), :] = w[level + 1, block(b), :] - lift
                else:
                    w[level + 1, block(b), :] = -lift
                if b == 0:
                    rows = slice(OFF + 2, OFF + 8)
                    grad = row_diff(p, level + 1, OFF + 2)[0:6, :]
                elif b == BLOCKS - 1:
                    rows = slice(OFF + CX - 8, OFF + CX - 2)
                    grad = row_diff(p, level + 1, OFF + CX - 10)[2:8, :]
                else:
                    rows = padded(b)
                    grad = row_diff(p, level + 1, OFF + 8 * b)
                u[level, rows, :] = u[level, rows, :] - bo[rows, :] * grad
        return 0

    lax.fori_loop(0, LEV // BATCH, motion, 0)

    def change(index, _):
        base = index * BATCH
        slope = lane_diff(v[pl.ds(base, BATCH)].reshape(BATCH * CX, CY), taps)
        for b in range(BLOCKS):
            for i in range(BATCH):
                level = base + i
                div = slope[i * CX + 8 * b : i * CX + 8 * b + 8, :]
                div = div + (w[level + 2, block(b), :] - w[level, block(b), :])
                if 0 < b < BLOCKS - 1:
                    div = div + row_diff(u, level, OFF + 8 * b)
                new_p = p[level + 1, padded(b), :] - bk[block(b), :] * div
                new_p = new_p + sc[pl.ds(level, 1), :] * w[level + 1, block(b), :]
                if 0 < b < BLOCKS - 1:
                    p[level + 1, padded(b), :] = new_p
                else:
                    rest[level, block(min(b, 1)), :] = new_p
        return 0

    lax.fori_loop(0, LEV // BATCH, change, 0)


def sensor_kernel(table, inj):
    me = lax.axis_index("dip").astype(F32)
    lane = lanes((1, CY))
    for k in range(STEPS):
        for b in range(BLOCKS):
            inj[k, block(b), :] = jnp.zeros((8, CY), F32)

    def one(d, _):
        for i in range(8):
            keep = jnp.where(table[d, 32 + i] == me, 1.0, 0.0)
            row = table[d, 40 + i].astype(jnp.int32)
            hit = lane == table[d, 48 + i].astype(jnp.int32)
            for k in range(STEPS):
                add = jnp.where(hit, table[d, 8 * k + i] * keep, 0.0)
                inj[k, pl.ds(row, 1), :] = inj[k, pl.ds(row, 1), :] + add
        return 0

    lax.fori_loop(0, 8, one, 0)


def outer_kernel(step, part, *refs):
    head, tail = step == 0, step == STEPS - 1
    deepest = part in (None, GROUPS - 1)
    start, stop = (0, LEV) if part is None else (16 * part, 16 * part + 16)
    blocks = (0, GROUPS) if part is None else (part, part + 1)
    refs = list(refs)
    take = lambda n: [refs.pop(0) for _ in range(n)]
    bk, inj, rest, own, from_up, from_down, from_left, from_right = take(8)
    _, _, _ = take(3)
    if tail:
        bo_a, bo_b, bo_c, va, vb, vc = take(6)
        if not deepest:
            take(1)
        p, u, bo, out = take(4)
        floor = take(1)[0] if deepest else None
        fix, taps, fresh, sems = take(4)
    elif not head:
        bo_a, bo_b, bo_c = take(3)
        _, _, _ = take(3)
    if not tail:
        p, u, bo = take(3)
    if head:
        bo_a, bo_b, bo_c = take(3)
    if not tail:
        va, vb, vc = take(3)
        last, first, side = take(3)
        fix, taps = take(2)
    fill_taps(taps)

    strike, dip = lax.axis_index("strike"), lax.axis_index("dip")
    keep_up = jnp.where(strike > 0, 1.0, 0.0)
    keep_down = jnp.where(strike < lax.axis_size("strike") - 1, 1.0, 0.0)
    keep_left = jnp.where(dip > 0, 1.0, 0.0)
    keep_right = jnp.where(dip < lax.axis_size("dip") - 1, 1.0, 0.0)

    def halo(level, _):
        p[level + 1, OFF - 4 : OFF, :] = from_up[level, :, :] * keep_up
        p[level + 1, OFF + CX : OFF + CX + 4, :] = from_down[level, :, :] * keep_down
        return 0

    lax.fori_loop(start, stop, halo, 0, unroll=8)

    spot = lanes((CX, CY)) & 7
    low_half = spot < 4
    if head:

        def halo_u(pair, _):
            for half in range(2):
                here = slice(2 * half, 2 * half + 2)
                level = 2 * pair + half
                u[level, OFF - 2 : OFF, :] = from_up[LEV + pair, here, :] * keep_up
                u[level, OFF + CX : OFF + CX + 2, :] = from_down[LEV + pair, here, :] * keep_down
            return 0

        lax.fori_loop(0, LEV // 2, halo_u, 0, unroll=4)
        bo[OFF - 2 : OFF, :] = from_up[LEV + LEV // 2, 0:2, :] * keep_up
        bo[OFF + CX : OFF + CX + 2, :] = from_down[LEV + LEV // 2, 0:2, :] * keep_down
        mine = own[2 * GROUPS]
        bo_a[...] = jnp.where(low_half, from_left[2 * GROUPS] * keep_left, mine)
        bo_b[...] = jnp.where(low_half, mine, from_right[2 * GROUPS] * keep_right)
        bo_c[...] = mine
        for g in range(GROUPS):
            mine = own[GROUPS + g]
            va[g] = jnp.where(low_half, from_left[GROUPS + g] * keep_left, mine)
            vb[g] = jnp.where(low_half, mine, from_right[GROUPS + g] * keep_right)
            vc[g] = mine

    def sides(g, _):
        middle = (spot >= 2) & (spot < 6)
        mine = own[g]
        a = jnp.where(low_half, from_left[g] * keep_left, mine)
        c = jnp.where(low_half, mine, from_right[g] * keep_right)
        turn = lane_diff(jnp.concatenate([a, c, mine], axis=0), taps)
        new_a = va[g] - bo_a[...] * turn[0:CX]
        new_b = vb[g] - bo_b[...] * turn[CX : 2 * CX]
        new_c = vc[g] - bo_c[...] * turn[2 * CX : 3 * CX]
        if not tail:
            va[g] = new_a
            vb[g] = new_b
            vc[g] = new_c
        rest = jnp.concatenate(
            [
                jnp.where(middle, new_a - new_c, 0.0),
                jnp.where(middle, new_b - new_c, 0.0),
            ],
            axis=0,
        )
        turn = lane_diff(rest, taps)
        fix[g] = jnp.where(low_half, turn[CX : 2 * CX], turn[0:CX])
        return 0

    lax.fori_loop(*blocks, sides, 0)

    def rims(level, _):
        for row in (OFF - 2, OFF + CX - 2):
            rows = slice(row, row + 4)
            grad = row_diff(p, level + 1, row - 2)[2:6, :]
            u[level, rows, :] = u[level, rows, :] - bo[rows, :] * grad
        return 0

    lax.fori_loop(start, stop, rims, 0, unroll=8)

    lane = lanes()
    edge = (lane < 4) | (lane >= CY - 4)
    group_of = lane >> 3

    def one(group, _):
        for b in range(BLOCKS):
            at = block(b)
            gain = bk[at, :]
            sides_gain = jnp.where(edge, gain, 0.0)
            spread = fix[group, at, :]
            packed = jnp.zeros((8, CY), F32)
            for j in range(16):
                level = group * 16 + j
                new_p = sides_gain * rolled(spread, -(8 * j + 4))
                if 0 < b < BLOCKS - 1:
                    new_p = p[level + 1, padded(b), :] - new_p
                else:
                    new_p = rest[level, block(min(b, 1)), :] - new_p
                    new_p = new_p - gain * row_diff(u, level, OFF + 8 * b)
                if deepest and j == 15:
                    here = jnp.where(group == GROUPS - 1, 1.0, 0.0)
                    new_p = new_p + here * inj[step, at, :]
                if tail:
                    fresh[j, at, :] = new_p
                else:
                    p[level + 1, padded(b), :] = new_p
                    packed = jnp.where(group_of == j, rolled(new_p, 8 * j + 4), packed)
                    if b == 0:
                        first[level, :, :] = new_p[0:4, :]
                    if b == BLOCKS - 1:
                        last[level, :, :] = new_p[4:8, :]
            if not tail:
                side[group, at, :] = packed
        if tail:
            copy = pltpu.make_async_copy(fresh, out.at[pl.ds(group * 16, 16)], sems.at[0])
            copy.start()
        return 0

    if tail:
        one(part, 0)
        if deepest:
            floor[...] = fresh[15]
        pltpu.make_async_copy(fresh, out.at[pl.ds(part * 16, 16)], sems.at[0]).wait()
    else:
        lax.fori_loop(0, GROUPS, one, 0)


def kept(*arrays):
    space = pltpu.MemorySpace.HBM
    return [pltpu.with_memory_space_constraint(x, space) for x in arrays]


def shaped(*shape):
    return jax.ShapeDtypeStruct(shape, F32)


def params(mib):
    return pltpu.CompilerParams(vmem_limit_bytes=mib << 20)


def cost(mib):
    return pl.CostEstimate(flops=20_000_000, bytes_accessed=mib << 20, transcendentals=0)


P_SHAPE = shaped(LEV + 2, ROWS, CY)
U_SHAPE = shaped(LEV, ROWS, CY)
V_SHAPE = shaped(LEV, CX, CY)
W_SHAPE = shaped(LEV + 2, CX, CY)
BO_SHAPE = shaped(ROWS, CY)
MAP = shaped(CX, CY)
TAPS = pltpu.VMEM((2 * CY, CY), jnp.bfloat16)
SIDE = shaped(GROUPS, CX, CY)
STRIP = shaped(LEV, 4, CY)


def prep(gravity, amp, owner, cell):
    return pl.pallas_call(
        prep_kernel,
        out_shape=(shaped(LEV, CY), shaped(8, CY)),
        in_specs=[ANY] * 4,
        out_specs=[VMEM] * 2,
        scratch_shapes=[
            pltpu.SMEM((LEV,), F32),
            pltpu.SMEM((STEPS, 8), F32),
            pltpu.SMEM((8,), jnp.int32),
            pltpu.SMEM((8,), jnp.int32),
            pltpu.SemaphoreType.DMA((4,)),
        ],
        compiler_params=params(4),
        name="prep",
    )(*kept(gravity, amp, owner, cell))


def load(bulk_t, buoy_t, bathy, p, u, v):
    wide = shaped(LEV + LEV // 2 + 1, 4, CY)
    return pl.pallas_call(
        load_kernel,
        out_shape=(
            P_SHAPE, U_SHAPE, V_SHAPE, BO_SHAPE, MAP, wide, wide,
            shaped(2 * GROUPS + 1, CX, CY),
        ),
        in_specs=[ANY] * 6,
        out_specs=[VMEM] * 8,
        scratch_shapes=[
            pltpu.SMEM((NCLASS,), F32),
            pltpu.SMEM((NCLASS,), F32),
            pltpu.VMEM((CX, CY), jnp.int32),
            pltpu.SemaphoreType.DMA((6,)),
        ],
        compiler_params=params(16),
        cost_estimate=cost(8),
        name="load",
    )(*kept(bulk_t, buoy_t, bathy, p, u, v))


def inner(sc, bk, bo, p, u, v, w):
    args = (sc, bk, bo, p, u, v) + (() if w is None else (w,))
    alias = {3: 0, 4: 1, 5: 2}
    if w is not None:
        alias[6] = 3
    return pl.pallas_call(
        functools.partial(inner_kernel, w is not None),
        out_shape=(P_SHAPE, U_SHAPE, V_SHAPE, W_SHAPE, shaped(LEV, 16, CY)),
        in_specs=[VMEM] * len(args),
        out_specs=[VMEM] * 5,
        scratch_shapes=[TAPS],
        input_output_aliases=alias,
        compiler_params=params(16),
        cost_estimate=cost(16),
        name="inner",
    )(*args)


def sensors(table):
    return pl.pallas_call(
        sensor_kernel,
        out_shape=shaped(STEPS, CX, CY),
        in_specs=[SMEM],
        out_specs=VMEM,
        compiler_params=params(4),
        name="sensors",
    )(table)


def outer(step, bk, inj, rest, own, up, down, left, right, p, u, bo, state):
    head = step == 0
    args = [bk, inj, rest, own, up, down, left, right, p, u, bo]
    shapes = [P_SHAPE, U_SHAPE, BO_SHAPE]
    alias = {8: 0, 9: 1, 10: 2}
    if head:
        shapes += [MAP, MAP, MAP, SIDE, SIDE, SIDE]
    else:
        args += list(state)
        shapes += [SIDE, SIDE, SIDE]
        alias.update({14: 3, 15: 4, 16: 5})
    shapes += [STRIP, STRIP, SIDE]
    return pl.pallas_call(
        functools.partial(outer_kernel, step, None),
        out_shape=tuple(shapes),
        in_specs=[VMEM] * len(args),
        out_specs=[VMEM] * len(shapes),
        scratch_shapes=[pltpu.VMEM((GROUPS, CX, CY), F32), TAPS],
        input_output_aliases=alias,
        compiler_params=params(20),
        cost_estimate=cost(12),
        name="outer",
    )(*args)


def finish(part, bk, inj, rest, own, up, down, left, right, p, u, bo, state, out):
    args = [bk, inj, rest, own, up, down, left, right, p, u, bo, *state]
    in_specs = [VMEM] * len(args)
    shapes = [P_SHAPE, U_SHAPE, BO_SHAPE, V_SHAPE]
    specs = [VMEM] * 3 + [ANY]
    alias = {8: 0, 9: 1, 10: 2}
    if out is None:
        shapes.append(MAP)
        specs.append(VMEM)
    else:
        alias[len(args)] = 3
        args.append(out)
        in_specs.append(ANY)
    return pl.pallas_call(
        functools.partial(outer_kernel, STEPS - 1, part),
        out_shape=tuple(shapes),
        in_specs=in_specs,
        out_specs=specs,
        scratch_shapes=[
            pltpu.VMEM((GROUPS, CX, CY), F32),
            TAPS,
            pltpu.VMEM((16, CX, CY), F32),
            pltpu.SemaphoreType.DMA((1,)),
        ],
        input_output_aliases=alias,
        compiler_params=params(16),
        cost_estimate=cost(6),
        name="finish",
    )(*args)


def ring(x, axis, by):
    n = lax.axis_size(axis)
    return lax.ppermute(x, axis, [(i, (i + by) % n) for i in range(n)])


def swap(x, axis, bit):
    n = lax.axis_size(axis)
    return lax.ppermute(x, axis, [(i, i ^ bit) for i in range(n)])


def body(
    pressure,
    strike_vel,
    dip_vel,
    bathy_class,
    bulk_table,
    buoy_table,
    gravity,
    sensor_amp,
    sensor_owner,
    sensor_cell,
    probe_kernel,
):
    strikes, dips = lax.axis_size("strike"), lax.axis_size("dip")
    sc, table = prep(gravity, sensor_amp, sensor_owner[:, 0], sensor_cell)
    for bit in (1, 2, 4):
        table = table + swap(table, "dip", bit)
    inj = sensors(table)

    p, u, v, bo, bk, last, first, side = load(
        bulk_table, buoy_table, bathy_class, pressure, strike_vel, dip_vel
    )
    w = None
    state = None
    for step in range(STEPS):
        up, down = ring(last, "strike", 1), ring(first, "strike", -1)
        left, right = ring(side, "dip", 1), ring(side, "dip", -1)
        p, u, v, w, rest = inner(sc, bk, bo, p, u, v, w)
        if step == STEPS - 1:
            break
        res = outer(step, bk, inj, rest, side, up, down, left, right, p, u, bo, state)
        p, u, bo = res[:3]
        if step == 0:
            state = res[3:9]
        else:
            state = state[:3] + res[3:6]
        last, first, side = res[-3:]

    def piece(part, p, u, bo, out):
        return finish(
            part, bk, inj, rest, side, up, down, left, right, p, u, bo, state, out
        )

    p, u, bo, out, seafloor = piece(GROUPS - 1, p, u, bo, None)
    cells = CX * CY
    total_cells = cells * strikes * dips
    scale = 1.0 / math.sqrt(total_cells)
    panel = (probe_kernel.astype(F32) * seafloor[None] * scale).reshape(PROBES, cells)
    gram = jnp.dot(panel, panel.T, precision=lax.Precision.HIGHEST)
    gram = gram + swap(gram, "dip", 1)
    part = GROUPS - 2
    for axis, stride in (("dip", 2), ("strike", 1), ("strike", 4)):
        pieces = [swap(gram, axis, stride * bits) for bits in (1, 2, 3)]
        gram, p = lax.optimization_barrier((gram, p))
        p, u, bo, out = piece(part, p, u, bo, out)
        part -= 1
        *pieces, p = lax.optimization_barrier((*pieces, p))
        gram = gram + sum(pieces)
    return (out, lax.linalg.cholesky(gram, symmetrize_input=False).T)


def solution(mesh):
    return jax.shard_map(
        body,
        mesh=mesh,
        in_specs=(
            P(None, "strike", "dip"),
            P(None, "strike", "dip"),
            P(None, "strike", "dip"),
            P("strike", "dip"),
            P(),
            P(),
            P(),
            P(None, ("strike", "dip")),
            P(("strike", "dip"), None),
            P(("strike", "dip")),
            P(None, "strike", "dip"),
        ),
        out_specs=(P(None, "strike", "dip"), P()),
        check_vma=False,
    )
```

```python
import functools
import math

import jax
import jax.numpy as jnp
from jax import lax
from jax.experimental import pallas as pl
from jax.experimental.pallas import tpu as pltpu
from jax.sharding import PartitionSpec as P

STEPS = 4
PROBES = 96
NCLASS = 8
LEV = 64
CX = 64
CY = 128
OFF = 8
ROWS = CX + 2 * OFF
GROUPS = LEV // 16
BLOCKS = CX // 8
BATCH = 16
time_step = 0.2

F32 = jnp.float32
VMEM = pl.BlockSpec(memory_space=pltpu.VMEM)
SMEM = pl.BlockSpec(memory_space=pltpu.SMEM)
ANY = pl.BlockSpec(memory_space=pltpu.MemorySpace.HBM)


def rolled(x, shift):
    return pltpu.roll(x, shift % CY, 1)


def lanes(shape=(8, CY)):
    return lax.broadcasted_iota(jnp.int32, shape, 1)


def lane_diff(x):
    return 8.0 * (rolled(x, -1) - rolled(x, 1)) - (rolled(x, -2) - rolled(x, 2))


def row_diff(ref, level, row):
    def at(shift):
        return ref[level, row + shift : row + shift + 8, :]

    return 8.0 * (at(1) - at(-1)) - (at(2) - at(-2))


def fill_taps(taps):
    shape = (2 * CY, CY)
    source = lax.broadcasted_iota(jnp.int32, shape, 0) & (CY - 1)
    ahead = (source - lax.broadcasted_iota(jnp.int32, shape, 1)) & (CY - 1)
    value = jnp.where(ahead == 1, 8.0, 0.0) - jnp.where(ahead == CY - 1, 8.0, 0.0)
    value = value - jnp.where(ahead == 2, 1.0, 0.0) + jnp.where(ahead == CY - 2, 1.0, 0.0)
    taps[...] = value.astype(jnp.bfloat16)


def lane_diff(x, taps):
    high = x.astype(jnp.bfloat16)
    low = (x - high.astype(F32)).astype(jnp.bfloat16)
    parts = jnp.concatenate([high, low], axis=1)
    return jnp.dot(parts, taps[...], preferred_element_type=F32)


def block(index):
    return slice(8 * index, 8 * index + 8)


def padded(index):
    return slice(OFF + 8 * index, OFF + 8 * index + 8)


def pack(src, src_level, dst, dst_base, src_off):
    group_of = lanes() >> 3

    def one(group, _):
        for b in range(BLOCKS):
            acc = jnp.zeros((8, CY), F32)
            for j in range(16):
                x = src[src_level + group * 16 + j, src_off + 8 * b : src_off + 8 * b + 8, :]
                acc = jnp.where(group_of == j, rolled(x, 8 * j + 4), acc)
            dst[dst_base + group, block(b), :] = acc
        return 0

    lax.fori_loop(0, GROUPS, one, 0)


def prep_kernel(gravity_h, amp_h, owner_h, cell_h, sc, table, gravity, amp, owner, cell, sems):
    pairs = ((gravity_h, gravity), (amp_h, amp), (owner_h, owner), (cell_h, cell))
    copies = [pltpu.make_async_copy(a, b, sems.at[i]) for i, (a, b) in enumerate(pairs)]
    for copy in copies:
        copy.start()
    dip = lax.axis_index("dip")
    lane, row = lanes((8, CY)), lax.broadcasted_iota(jnp.int32, (8, CY), 0)
    for copy in copies:
        copy.wait()
    for start in range(0, LEV, 8):
        part = jnp.zeros((8, CY), F32)
        for i in range(8):
            part = jnp.where(row == i, time_step / 6.0 * gravity[start + i], part)
        sc[start : start + 8, :] = part
    sheet = jnp.zeros((8, CY), F32)
    for i in range(8):
        for k in range(STEPS):
            sheet = jnp.where(lane == 8 * k + i, amp[k, i], sheet)
        sheet = jnp.where(lane == 32 + i, owner[i].astype(F32), sheet)
        sheet = jnp.where(lane == 40 + i, (cell[i] // CY).astype(F32), sheet)
        sheet = jnp.where(lane == 48 + i, (cell[i] % CY).astype(F32), sheet)
    table[...] = jnp.where(row == dip, sheet, 0.0)


def load_kernel(
    bulk_h, buoy_h, bathy_h, p_hbm, u_hbm, v_hbm, p, u, v, bo, bk, last, first, side,
    bulk_t, buoy_t, bathy, sems
):
    small = [
        pltpu.make_async_copy(bathy_h, bathy, sems.at[3]),
        pltpu.make_async_copy(bulk_h, bulk_t, sems.at[4]),
        pltpu.make_async_copy(buoy_h, buoy_t, sems.at[5]),
    ]
    for copy in small:
        copy.start()
    copies = [
        pltpu.make_async_copy(p_hbm, p.at[1 : LEV + 1, OFF : OFF + CX, :], sems.at[0]),
        pltpu.make_async_copy(v_hbm, v, sems.at[1]),
        pltpu.make_async_copy(u_hbm, u.at[:, OFF : OFF + CX, :], sems.at[2]),
    ]
    for copy in copies:
        copy.start()
    zero = jnp.zeros((8, CY), F32)
    for level in (0, LEV + 1):
        for b in range(ROWS // 8):
            p[level, block(b), :] = zero
    group_of = lanes() >> 3
    for copy in small:
        copy.wait()
    bo[0:8, :] = zero
    bo[ROWS - 8 : ROWS, :] = zero
    for b in range(BLOCKS):
        label = bathy[block(b), :]
        bulk = zero
        buoy = zero
        for c in range(NCLASS):
            bulk = jnp.where(label == c, bulk_t[c], bulk)
            buoy = jnp.where(label == c, buoy_t[c], buoy)
        buoy = buoy * (time_step / 12.0)
        bk[block(b), :] = bulk * (time_step / 12.0)
        bo[padded(b), :] = buoy
        acc = zero
        for j in range(16):
            acc = jnp.where(group_of == j, rolled(buoy, 8 * j + 4), acc)
        side[2 * GROUPS, block(b), :] = acc
    copies[0].wait()
    pack(p, 1, side, 0, OFF)

    def strip(level, _):
        first[level, :, :] = p[level + 1, OFF : OFF + 4, :]
        last[level, :, :] = p[level + 1, OFF + CX - 4 : OFF + CX, :]
        return 0

    lax.fori_loop(0, LEV, strip, 0, unroll=8)
    copies[1].wait()
    pack(v, 0, side, GROUPS, 0)
    copies[2].wait()

    def strip_u(pair, _):
        for half in range(2):
            here = slice(2 * half, 2 * half + 2)
            first[LEV + pair, here, :] = u[2 * pair + half, OFF : OFF + 2, :]
            last[LEV + pair, here, :] = u[2 * pair + half, OFF + CX - 2 : OFF + CX, :]
        return 0

    lax.fori_loop(0, LEV // 2, strip_u, 0, unroll=4)
    first[LEV + LEV // 2, 0:2, :] = bo[OFF : OFF + 2, :]
    last[LEV + LEV // 2, 0:2, :] = bo[OFF + CX - 2 : OFF + CX, :]
    first[LEV + LEV // 2, 2:4, :] = jnp.zeros((2, CY), F32)
    last[LEV + LEV // 2, 2:4, :] = jnp.zeros((2, CY), F32)


def inner_kernel(started, *refs):
    sc, bk, bo = refs[:3]
    p, u, v, w, rest, taps = refs[-6:]
    if not started:
        for b in range(BLOCKS):
            w[0, block(b), :] = jnp.zeros((8, CY), F32)
            w[LEV + 1, block(b), :] = jnp.zeros((8, CY), F32)
    fill_taps(taps)

    def motion(index, _):
        base = index * BATCH
        field = p[pl.ds(base + 1, BATCH), OFF : OFF + CX, :].reshape(BATCH * CX, CY)
        slope = lane_diff(field, taps)
        for b in range(BLOCKS):
            coef = bo[padded(b), :]
            lines = [p[base + i, padded(b), :] for i in range(BATCH + 2)]
            for i in range(BATCH):
                level = base + i
                part = slope[i * CX + 8 * b : i * CX + 8 * b + 8, :]
                v[level, block(b), :] = v[level, block(b), :] - coef * part
                lift = (36.0 * coef) * (lines[i + 2] - lines[i])
                if started:
                    w[level + 1, block(b), :] = w[level + 1, block(b), :] - lift
                else:
                    w[level + 1, block(b), :] = -lift
                if b == 0:
                    rows = slice(OFF + 2, OFF + 8)
                    grad = row_diff(p, level + 1, OFF + 2)[0:6, :]
                elif b == BLOCKS - 1:
                    rows = slice(OFF + CX - 8, OFF + CX - 2)
                    grad = row_diff(p, level + 1, OFF + CX - 10)[2:8, :]
                else:
                    rows = padded(b)
                    grad = row_diff(p, level + 1, OFF + 8 * b)
                u[level, rows, :] = u[level, rows, :] - bo[rows, :] * grad
        return 0

    lax.fori_loop(0, LEV // BATCH, motion, 0)

    def change(index, _):
        base = index * BATCH
        slope = lane_diff(v[pl.ds(base, BATCH)].reshape(BATCH * CX, CY), taps)
        for b in range(BLOCKS):
            for i in range(BATCH):
                level = base + i
                div = slope[i * CX + 8 * b : i * CX + 8 * b + 8, :]
                div = div + (w[level + 2, block(b), :] - w[level, block(b), :])
                if 0 < b < BLOCKS - 1:
                    div = div + row_diff(u, level, OFF + 8 * b)
                new_p = p[level + 1, padded(b), :] - bk[block(b), :] * div
                new_p = new_p + sc[pl.ds(level, 1), :] * w[level + 1, block(b), :]
                if 0 < b < BLOCKS - 1:
                    p[level + 1, padded(b), :] = new_p
                else:
                    rest[level, block(min(b, 1)), :] = new_p
        return 0

    lax.fori_loop(0, LEV // BATCH, change, 0)


def sensor_kernel(table, inj):
    me = lax.axis_index("dip").astype(F32)
    lane = lanes((1, CY))
    for k in range(STEPS):
        for b in range(BLOCKS):
            inj[k, block(b), :] = jnp.zeros((8, CY), F32)

    def one(d, _):
        for i in range(8):
            keep = jnp.where(table[d, 32 + i] == me, 1.0, 0.0)
            row = table[d, 40 + i].astype(jnp.int32)
            hit = lane == table[d, 48 + i].astype(jnp.int32)
            for k in range(STEPS):
                add = jnp.where(hit, table[d, 8 * k + i] * keep, 0.0)
                inj[k, pl.ds(row, 1), :] = inj[k, pl.ds(row, 1), :] + add
        return 0

    lax.fori_loop(0, 8, one, 0)


def outer_kernel(step, part, *refs):
    head, tail = step == 0, step == STEPS - 1
    deepest = part in (None, GROUPS - 1)
    start, stop = (0, LEV) if part is None else (16 * part, 16 * part + 16)
    blocks = (0, GROUPS) if part is None else (part, part + 1)
    refs = list(refs)
    take = lambda n: [refs.pop(0) for _ in range(n)]
    bk, inj, rest, own, from_up, from_down, from_left, from_right = take(8)
    _, _, _ = take(3)
    if tail:
        bo_a, bo_b, bo_c, va, vb, vc = take(6)
        if not deepest:
            take(1)
        p, u, bo, out = take(4)
        floor = take(1)[0] if deepest else None
        fix, taps, fresh, sems = take(4)
    elif not head:
        bo_a, bo_b, bo_c = take(3)
        _, _, _ = take(3)
    if not tail:
        p, u, bo = take(3)
    if head:
        bo_a, bo_b, bo_c = take(3)
    if not tail:
        va, vb, vc = take(3)
        last, first, side = take(3)
        fix, taps = take(2)
    fill_taps(taps)

    strike, dip = lax.axis_index("strike"), lax.axis_index("dip")
    keep_up = jnp.where(strike > 0, 1.0, 0.0)
    keep_down = jnp.where(strike < lax.axis_size("strike") - 1, 1.0, 0.0)
    keep_left = jnp.where(dip > 0, 1.0, 0.0)
    keep_right = jnp.where(dip < lax.axis_size("dip") - 1, 1.0, 0.0)

    def halo(level, _):
        p[level + 1, OFF - 4 : OFF, :] = from_up[level, :, :] * keep_up
        p[level + 1, OFF + CX : OFF + CX + 4, :] = from_down[level, :, :] * keep_down
        return 0

    lax.fori_loop(start, stop, halo, 0, unroll=8)

    spot = lanes((CX, CY)) & 7
    low_half = spot < 4
    if head:

        def halo_u(pair, _):
            for half in range(2):
                here = slice(2 * half, 2 * half + 2)
                level = 2 * pair + half
                u[level, OFF - 2 : OFF, :] = from_up[LEV + pair, here, :] * keep_up
                u[level, OFF + CX : OFF + CX + 2, :] = from_down[LEV + pair, here, :] * keep_down
            return 0

        lax.fori_loop(0, LEV // 2, halo_u, 0, unroll=4)
        bo[OFF - 2 : OFF, :] = from_up[LEV + LEV // 2, 0:2, :] * keep_up
        bo[OFF + CX : OFF + CX + 2, :] = from_down[LEV + LEV // 2, 0:2, :] * keep_down
        mine = own[2 * GROUPS]
        bo_a[...] = jnp.where(low_half, from_left[2 * GROUPS] * keep_left, mine)
        bo_b[...] = jnp.where(low_half, mine, from_right[2 * GROUPS] * keep_right)
        bo_c[...] = mine
        for g in range(GROUPS):
            mine = own[GROUPS + g]
            va[g] = jnp.where(low_half, from_left[GROUPS + g] * keep_left, mine)
            vb[g] = jnp.where(low_half, mine, from_right[GROUPS + g] * keep_right)
            vc[g] = mine

    middle = (spot >= 2) & (spot < 6)
    fields = []
    for g in range(*blocks):
        mine = own[g]
        fields.append(jnp.where(low_half, from_left[g] * keep_left, mine))
        fields.append(jnp.where(low_half, mine, from_right[g] * keep_right))
        fields.append(mine)
    turn = lane_diff(jnp.concatenate(fields, axis=0), taps)
    fields = []
    for n, g in enumerate(range(*blocks)):
        at = 3 * n * CX
        new_a = va[g] - bo_a[...] * turn[at : at + CX]
        new_b = vb[g] - bo_b[...] * turn[at + CX : at + 2 * CX]
        new_c = vc[g] - bo_c[...] * turn[at + 2 * CX : at + 3 * CX]
        if not tail:
            va[g] = new_a
            vb[g] = new_b
            vc[g] = new_c
        fields.append(jnp.where(middle, new_a - new_c, 0.0))
        fields.append(jnp.where(middle, new_b - new_c, 0.0))
    turn = lane_diff(jnp.concatenate(fields, axis=0), taps)
    for n, g in enumerate(range(*blocks)):
        at = 2 * n * CX
        fix[g] = jnp.where(low_half, turn[at + CX : at + 2 * CX], turn[at : at + CX])

    def rims(level, _):
        for row in (OFF - 2, OFF + CX - 2):
            rows = slice(row, row + 4)
            grad = row_diff(p, level + 1, row - 2)[2:6, :]
            u[level, rows, :] = u[level, rows, :] - bo[rows, :] * grad
        return 0

    lax.fori_loop(start, stop, rims, 0, unroll=8)

    lane = lanes()
    edge = (lane < 4) | (lane >= CY - 4)
    group_of = lane >> 3

    def one(group, _):
        for b in range(BLOCKS):
            at = block(b)
            gain = bk[at, :]
            sides_gain = jnp.where(edge, gain, 0.0)
            spread = fix[group, at, :]
            packed = jnp.zeros((8, CY), F32)
            for j in range(16):
                level = group * 16 + j
                new_p = sides_gain * rolled(spread, -(8 * j + 4))
                if 0 < b < BLOCKS - 1:
                    new_p = p[level + 1, padded(b), :] - new_p
                else:
                    new_p = rest[level, block(min(b, 1)), :] - new_p
                    new_p = new_p - gain * row_diff(u, level, OFF + 8 * b)
                if deepest and j == 15:
                    here = jnp.where(group == GROUPS - 1, 1.0, 0.0)
                    new_p = new_p + here * inj[step, at, :]
                if tail:
                    fresh[j, at, :] = new_p
                else:
                    p[level + 1, padded(b), :] = new_p
                    packed = jnp.where(group_of == j, rolled(new_p, 8 * j + 4), packed)
                    if b == 0:
                        first[level, :, :] = new_p[0:4, :]
                    if b == BLOCKS - 1:
                        last[level, :, :] = new_p[4:8, :]
            if not tail:
                side[group, at, :] = packed
        if tail:
            copy = pltpu.make_async_copy(fresh, out.at[pl.ds(group * 16, 16)], sems.at[0])
            copy.start()
        return 0

    if tail:
        one(part, 0)
        if deepest:
            floor[...] = fresh[15]
        pltpu.make_async_copy(fresh, out.at[pl.ds(part * 16, 16)], sems.at[0]).wait()
    else:
        lax.fori_loop(0, GROUPS, one, 0)


def kept(*arrays):
    space = pltpu.MemorySpace.HBM
    return [pltpu.with_memory_space_constraint(x, space) for x in arrays]


def shaped(*shape):
    return jax.ShapeDtypeStruct(shape, F32)


def params(mib):
    return pltpu.CompilerParams(vmem_limit_bytes=mib << 20)


def cost(mib):
    return pl.CostEstimate(flops=20_000_000, bytes_accessed=mib << 20, transcendentals=0)


P_SHAPE = shaped(LEV + 2, ROWS, CY)
U_SHAPE = shaped(LEV, ROWS, CY)
V_SHAPE = shaped(LEV, CX, CY)
W_SHAPE = shaped(LEV + 2, CX, CY)
BO_SHAPE = shaped(ROWS, CY)
MAP = shaped(CX, CY)
TAPS = pltpu.VMEM((2 * CY, CY), jnp.bfloat16)
SIDE = shaped(GROUPS, CX, CY)
STRIP = shaped(LEV, 4, CY)


def prep(gravity, amp, owner, cell):
    return pl.pallas_call(
        prep_kernel,
        out_shape=(shaped(LEV, CY), shaped(8, CY)),
        in_specs=[ANY] * 4,
        out_specs=[VMEM] * 2,
        scratch_shapes=[
            pltpu.SMEM((LEV,), F32),
            pltpu.SMEM((STEPS, 8), F32),
            pltpu.SMEM((8,), jnp.int32),
            pltpu.SMEM((8,), jnp.int32),
            pltpu.SemaphoreType.DMA((4,)),
        ],
        compiler_params=params(4),
        name="prep",
    )(*kept(gravity, amp, owner, cell))


def load(bulk_t, buoy_t, bathy, p, u, v):
    wide = shaped(LEV + LEV // 2 + 1, 4, CY)
    return pl.pallas_call(
        load_kernel,
        out_shape=(
            P_SHAPE, U_SHAPE, V_SHAPE, BO_SHAPE, MAP, wide, wide,
            shaped(2 * GROUPS + 1, CX, CY),
        ),
        in_specs=[ANY] * 6,
        out_specs=[VMEM] * 8,
        scratch_shapes=[
            pltpu.SMEM((NCLASS,), F32),
            pltpu.SMEM((NCLASS,), F32),
            pltpu.VMEM((CX, CY), jnp.int32),
            pltpu.SemaphoreType.DMA((6,)),
        ],
        compiler_params=params(16),
        cost_estimate=cost(8),
        name="load",
    )(*kept(bulk_t, buoy_t, bathy, p, u, v))


def inner(sc, bk, bo, p, u, v, w):
    args = (sc, bk, bo, p, u, v) + (() if w is None else (w,))
    alias = {3: 0, 4: 1, 5: 2}
    if w is not None:
        alias[6] = 3
    return pl.pallas_call(
        functools.partial(inner_kernel, w is not None),
        out_shape=(P_SHAPE, U_SHAPE, V_SHAPE, W_SHAPE, shaped(LEV, 16, CY)),
        in_specs=[VMEM] * len(args),
        out_specs=[VMEM] * 5,
        scratch_shapes=[TAPS],
        input_output_aliases=alias,
        compiler_params=params(16),
        cost_estimate=cost(16),
        name="inner",
    )(*args)


def sensors(table):
    return pl.pallas_call(
        sensor_kernel,
        out_shape=shaped(STEPS, CX, CY),
        in_specs=[SMEM],
        out_specs=VMEM,
        compiler_params=params(4),
        name="sensors",
    )(table)


def outer(step, bk, inj, rest, own, up, down, left, right, p, u, bo, state):
    head = step == 0
    args = [bk, inj, rest, own, up, down, left, right, p, u, bo]
    shapes = [P_SHAPE, U_SHAPE, BO_SHAPE]
    alias = {8: 0, 9: 1, 10: 2}
    if head:
        shapes += [MAP, MAP, MAP, SIDE, SIDE, SIDE]
    else:
        args += list(state)
        shapes += [SIDE, SIDE, SIDE]
        alias.update({14: 3, 15: 4, 16: 5})
    shapes += [STRIP, STRIP, SIDE]
    return pl.pallas_call(
        functools.partial(outer_kernel, step, None),
        out_shape=tuple(shapes),
        in_specs=[VMEM] * len(args),
        out_specs=[VMEM] * len(shapes),
        scratch_shapes=[pltpu.VMEM((GROUPS, CX, CY), F32), TAPS],
        input_output_aliases=alias,
        compiler_params=params(20),
        cost_estimate=cost(12),
        name="outer",
    )(*args)


def finish(part, bk, inj, rest, own, up, down, left, right, p, u, bo, state, out):
    args = [bk, inj, rest, own, up, down, left, right, p, u, bo, *state]
    in_specs = [VMEM] * len(args)
    shapes = [P_SHAPE, U_SHAPE, BO_SHAPE, V_SHAPE]
    specs = [VMEM] * 3 + [ANY]
    alias = {8: 0, 9: 1, 10: 2}
    if out is None:
        shapes.append(MAP)
        specs.append(VMEM)
    else:
        alias[len(args)] = 3
        args.append(out)
        in_specs.append(ANY)
    return pl.pallas_call(
        functools.partial(outer_kernel, STEPS - 1, part),
        out_shape=tuple(shapes),
        in_specs=in_specs,
        out_specs=specs,
        scratch_shapes=[
            pltpu.VMEM((GROUPS, CX, CY), F32),
            TAPS,
            pltpu.VMEM((16, CX, CY), F32),
            pltpu.SemaphoreType.DMA((1,)),
        ],
        input_output_aliases=alias,
        compiler_params=params(16),
        cost_estimate=cost(6),
        name="finish",
    )(*args)


def ring(x, axis, by):
    n = lax.axis_size(axis)
    return lax.ppermute(x, axis, [(i, (i + by) % n) for i in range(n)])


def swap(x, axis, bit):
    n = lax.axis_size(axis)
    return lax.ppermute(x, axis, [(i, i ^ bit) for i in range(n)])


def weighted_gram(probes, weight):
    flat = probes.reshape(PROBES, CX * CY)
    rest = flat.astype(F32) * weight.reshape(1, CX * CY)
    parts = []
    for _ in range(3):
        part = lax.reduce_precision(rest, 8, 7)
        rest = rest - part
        parts.append(part.astype(jnp.bfloat16))
    both = jnp.concatenate(parts, axis=0)
    sums = lax.dot_general(
        flat, both, (((1,), (1,)), ((), ())), preferred_element_type=F32
    )
    return sums[:, :PROBES] + sums[:, PROBES : 2 * PROBES] + sums[:, 2 * PROBES :]


def body(
    pressure,
    strike_vel,
    dip_vel,
    bathy_class,
    bulk_table,
    buoy_table,
    gravity,
    sensor_amp,
    sensor_owner,
    sensor_cell,
    probe_kernel,
):
    strikes, dips = lax.axis_size("strike"), lax.axis_size("dip")
    sc, table = prep(gravity, sensor_amp, sensor_owner[:, 0], sensor_cell)
    for bit in (1, 2, 4):
        table = table + swap(table, "dip", bit)
    inj = sensors(table)

    p, u, v, bo, bk, last, first, side = load(
        bulk_table, buoy_table, bathy_class, pressure, strike_vel, dip_vel
    )
    w = None
    state = None
    for step in range(STEPS):
        up, down = ring(last, "strike", 1), ring(first, "strike", -1)
        left, right = ring(side, "dip", 1), ring(side, "dip", -1)
        p, u, v, w, rest = inner(sc, bk, bo, p, u, v, w)
        if step == STEPS - 1:
            break
        res = outer(step, bk, inj, rest, side, up, down, left, right, p, u, bo, state)
        p, u, bo = res[:3]
        if step == 0:
            state = res[3:9]
        else:
            state = state[:3] + res[3:6]
        last, first, side = res[-3:]

    def piece(part, p, u, bo, out):
        return finish(
            part, bk, inj, rest, side, up, down, left, right, p, u, bo, state, out
        )

    p, u, bo, out, seafloor = piece(GROUPS - 1, p, u, bo, None)
    cells = CX * CY
    total_cells = cells * strikes * dips
    scale = 1.0 / math.sqrt(total_cells)
    gram = weighted_gram(probe_kernel, (seafloor * scale) ** 2)
    gram = gram + swap(gram, "dip", 1)
    part = GROUPS - 2
    for axis, stride in (("dip", 2), ("strike", 1), ("strike", 4)):
        pieces = [swap(gram, axis, stride * bits) for bits in (1, 2, 3)]
        gram, p = lax.optimization_barrier((gram, p))
        p, u, bo, out = piece(part, p, u, bo, out)
        part -= 1
        *pieces, p = lax.optimization_barrier((*pieces, p))
        gram = gram + sum(pieces)
    return (out, lax.linalg.cholesky(gram, symmetrize_input=False).T)


def solution(mesh):
    return jax.shard_map(
        body,
        mesh=mesh,
        in_specs=(
            P(None, "strike", "dip"),
            P(None, "strike", "dip"),
            P(None, "strike", "dip"),
            P("strike", "dip"),
            P(),
            P(),
            P(),
            P(None, ("strike", "dip")),
            P(("strike", "dip"), None),
            P(("strike", "dip")),
            P(None, "strike", "dip"),
        ),
        out_specs=(P(None, "strike", "dip"), P()),
        check_vma=False,
    )
```

```python
import functools
import math

import jax
import jax.numpy as jnp
from jax import lax
from jax.experimental import pallas as pl
from jax.experimental.pallas import tpu as pltpu
from jax.sharding import PartitionSpec as P

STEPS = 4
PROBES = 96
NCLASS = 8
LEV = 64
CX = 64
CY = 128
OFF = 8
ROWS = CX + 2 * OFF
GROUPS = LEV // 16
BLOCKS = CX // 8
BATCH = 16
time_step = 0.2

F32 = jnp.float32
VMEM = pl.BlockSpec(memory_space=pltpu.VMEM)
SMEM = pl.BlockSpec(memory_space=pltpu.SMEM)
ANY = pl.BlockSpec(memory_space=pltpu.MemorySpace.HBM)


def rolled(x, shift):
    return pltpu.roll(x, shift % CY, 1)


def lanes(shape=(8, CY)):
    return lax.broadcasted_iota(jnp.int32, shape, 1)


def lane_diff(x):
    return 8.0 * (rolled(x, -1) - rolled(x, 1)) - (rolled(x, -2) - rolled(x, 2))


def row_diff(ref, level, row):
    def at(shift):
        return ref[level, row + shift : row + shift + 8, :]

    return 8.0 * (at(1) - at(-1)) - (at(2) - at(-2))


def fill_taps(taps):
    shape = (2 * CY, CY)
    source = lax.broadcasted_iota(jnp.int32, shape, 0) & (CY - 1)
    ahead = (source - lax.broadcasted_iota(jnp.int32, shape, 1)) & (CY - 1)
    value = jnp.where(ahead == 1, 8.0, 0.0) - jnp.where(ahead == CY - 1, 8.0, 0.0)
    value = value - jnp.where(ahead == 2, 1.0, 0.0) + jnp.where(ahead == CY - 2, 1.0, 0.0)
    taps[...] = value.astype(jnp.bfloat16)


def lane_diff(x, taps):
    high = x.astype(jnp.bfloat16)
    low = (x - high.astype(F32)).astype(jnp.bfloat16)
    parts = jnp.concatenate([high, low], axis=1)
    return jnp.dot(parts, taps[...], preferred_element_type=F32)


def block(index):
    return slice(8 * index, 8 * index + 8)


def padded(index):
    return slice(OFF + 8 * index, OFF + 8 * index + 8)


def pack(src, src_level, dst, dst_base, src_off):
    group_of = lanes() >> 3

    def one(group, _):
        for b in range(BLOCKS):
            acc = jnp.zeros((8, CY), F32)
            for j in range(16):
                x = src[src_level + group * 16 + j, src_off + 8 * b : src_off + 8 * b + 8, :]
                acc = jnp.where(group_of == j, rolled(x, 8 * j + 4), acc)
            dst[dst_base + group, block(b), :] = acc
        return 0

    lax.fori_loop(0, GROUPS, one, 0)


def prep_kernel(gravity_h, amp_h, owner_h, cell_h, sc, table, gravity, amp, owner, cell, sems):
    pairs = ((gravity_h, gravity), (amp_h, amp), (owner_h, owner), (cell_h, cell))
    copies = [pltpu.make_async_copy(a, b, sems.at[i]) for i, (a, b) in enumerate(pairs)]
    for copy in copies:
        copy.start()
    dip = lax.axis_index("dip")
    lane, row = lanes((8, CY)), lax.broadcasted_iota(jnp.int32, (8, CY), 0)
    for copy in copies:
        copy.wait()
    for start in range(0, LEV, 8):
        part = jnp.zeros((8, CY), F32)
        for i in range(8):
            part = jnp.where(row == i, time_step / 6.0 * gravity[start + i], part)
        sc[start : start + 8, :] = part
    sheet = jnp.zeros((8, CY), F32)
    for i in range(8):
        for k in range(STEPS):
            sheet = jnp.where(lane == 8 * k + i, amp[k, i], sheet)
        sheet = jnp.where(lane == 32 + i, owner[i].astype(F32), sheet)
        sheet = jnp.where(lane == 40 + i, (cell[i] // CY).astype(F32), sheet)
        sheet = jnp.where(lane == 48 + i, (cell[i] % CY).astype(F32), sheet)
    table[...] = jnp.where(row == dip, sheet, 0.0)


def load_kernel(
    bulk_h, buoy_h, bathy_h, p_hbm, u_hbm, v_hbm, p, u, v, bo, bk, last, first, side,
    bulk_t, buoy_t, bathy, sems
):
    small = [
        pltpu.make_async_copy(bathy_h, bathy, sems.at[3]),
        pltpu.make_async_copy(bulk_h, bulk_t, sems.at[4]),
        pltpu.make_async_copy(buoy_h, buoy_t, sems.at[5]),
    ]
    for copy in small:
        copy.start()
    copies = [
        pltpu.make_async_copy(p_hbm, p.at[1 : LEV + 1, OFF : OFF + CX, :], sems.at[0]),
        pltpu.make_async_copy(v_hbm, v, sems.at[1]),
        pltpu.make_async_copy(u_hbm, u.at[:, OFF : OFF + CX, :], sems.at[2]),
    ]
    for copy in copies:
        copy.start()
    zero = jnp.zeros((8, CY), F32)
    for level in (0, LEV + 1):
        for b in range(ROWS // 8):
            p[level, block(b), :] = zero
    group_of = lanes() >> 3
    for copy in small:
        copy.wait()
    bo[0:8, :] = zero
    bo[ROWS - 8 : ROWS, :] = zero
    for b in range(BLOCKS):
        label = bathy[block(b), :]
        bulk = zero
        buoy = zero
        for c in range(NCLASS):
            bulk = jnp.where(label == c, bulk_t[c], bulk)
            buoy = jnp.where(label == c, buoy_t[c], buoy)
        buoy = buoy * (time_step / 12.0)
        bk[block(b), :] = bulk * (time_step / 12.0)
        bo[padded(b), :] = buoy
        acc = zero
        for j in range(16):
            acc = jnp.where(group_of == j, rolled(buoy, 8 * j + 4), acc)
        side[2 * GROUPS, block(b), :] = acc
    copies[0].wait()
    pack(p, 1, side, 0, OFF)

    def strip(level, _):
        first[level, :, :] = p[level + 1, OFF : OFF + 4, :]
        last[level, :, :] = p[level + 1, OFF + CX - 4 : OFF + CX, :]
        return 0

    lax.fori_loop(0, LEV, strip, 0, unroll=8)
    copies[1].wait()
    pack(v, 0, side, GROUPS, 0)
    copies[2].wait()

    def strip_u(pair, _):
        for half in range(2):
            here = slice(2 * half, 2 * half + 2)
            first[LEV + pair, here, :] = u[2 * pair + half, OFF : OFF + 2, :]
            last[LEV + pair, here, :] = u[2 * pair + half, OFF + CX - 2 : OFF + CX, :]
        return 0

    lax.fori_loop(0, LEV // 2, strip_u, 0, unroll=4)
    first[LEV + LEV // 2, 0:2, :] = bo[OFF : OFF + 2, :]
    last[LEV + LEV // 2, 0:2, :] = bo[OFF + CX - 2 : OFF + CX, :]
    first[LEV + LEV // 2, 2:4, :] = jnp.zeros((2, CY), F32)
    last[LEV + LEV // 2, 2:4, :] = jnp.zeros((2, CY), F32)


def inner_kernel(started, *refs):
    sc, bk, bo = refs[:3]
    p, u, v, w, rest, taps = refs[-6:]
    if not started:
        for b in range(BLOCKS):
            w[0, block(b), :] = jnp.zeros((8, CY), F32)
            w[LEV + 1, block(b), :] = jnp.zeros((8, CY), F32)
    fill_taps(taps)

    def motion(index, _):
        base = index * BATCH
        field = p[pl.ds(base + 1, BATCH), OFF : OFF + CX, :].reshape(BATCH * CX, CY)
        slope = lane_diff(field, taps)
        for b in range(BLOCKS):
            coef = bo[padded(b), :]
            lines = [p[base + i, padded(b), :] for i in range(BATCH + 2)]
            for i in range(BATCH):
                level = base + i
                part = slope[i * CX + 8 * b : i * CX + 8 * b + 8, :]
                v[level, block(b), :] = v[level, block(b), :] - coef * part
                lift = (36.0 * coef) * (lines[i + 2] - lines[i])
                if started:
                    w[level + 1, block(b), :] = w[level + 1, block(b), :] - lift
                else:
                    w[level + 1, block(b), :] = -lift
                if b == 0:
                    rows = slice(OFF + 2, OFF + 8)
                    grad = row_diff(p, level + 1, OFF + 2)[0:6, :]
                elif b == BLOCKS - 1:
                    rows = slice(OFF + CX - 8, OFF + CX - 2)
                    grad = row_diff(p, level + 1, OFF + CX - 10)[2:8, :]
                else:
                    rows = padded(b)
                    grad = row_diff(p, level + 1, OFF + 8 * b)
                u[level, rows, :] = u[level, rows, :] - bo[rows, :] * grad
        return 0

    lax.fori_loop(0, LEV // BATCH, motion, 0)

    def change(index, _):
        base = index * BATCH
        slope = lane_diff(v[pl.ds(base, BATCH)].reshape(BATCH * CX, CY), taps)
        for b in range(BLOCKS):
            for i in range(BATCH):
                level = base + i
                div = slope[i * CX + 8 * b : i * CX + 8 * b + 8, :]
                div = div + (w[level + 2, block(b), :] - w[level, block(b), :])
                if 0 < b < BLOCKS - 1:
                    div = div + row_diff(u, level, OFF + 8 * b)
                new_p = p[level + 1, padded(b), :] - bk[block(b), :] * div
                new_p = new_p + sc[pl.ds(level, 1), :] * w[level + 1, block(b), :]
                if 0 < b < BLOCKS - 1:
                    p[level + 1, padded(b), :] = new_p
                else:
                    rest[level, block(min(b, 1)), :] = new_p
        return 0

    lax.fori_loop(0, LEV // BATCH, change, 0)


def sensor_kernel(table, inj):
    me = lax.axis_index("dip").astype(F32)
    lane = lanes((1, CY))
    for k in range(STEPS):
        for b in range(BLOCKS):
            inj[k, block(b), :] = jnp.zeros((8, CY), F32)

    def one(d, _):
        for i in range(8):
            keep = jnp.where(table[d, 32 + i] == me, 1.0, 0.0)
            row = table[d, 40 + i].astype(jnp.int32)
            hit = lane == table[d, 48 + i].astype(jnp.int32)
            for k in range(STEPS):
                add = jnp.where(hit, table[d, 8 * k + i] * keep, 0.0)
                inj[k, pl.ds(row, 1), :] = inj[k, pl.ds(row, 1), :] + add
        return 0

    lax.fori_loop(0, 8, one, 0)


def outer_kernel(step, part, *refs):
    head, tail = step == 0, step == STEPS - 1
    deepest = part in (None, GROUPS - 1)
    start, stop = (0, LEV) if part is None else (16 * part, 16 * part + 16)
    blocks = (0, GROUPS) if part is None else (part, part + 1)
    refs = list(refs)
    take = lambda n: [refs.pop(0) for _ in range(n)]
    bk, inj, rest, own, from_up, from_down, from_left, from_right = take(8)
    _, _, _ = take(3)
    if tail:
        bo_a, bo_b, bo_c, va, vb, vc = take(6)
        if not deepest:
            take(1)
        p, u, bo, out = take(4)
        floor = take(1)[0] if deepest else None
        fix, taps, fresh, sems = take(4)
    elif not head:
        bo_a, bo_b, bo_c = take(3)
        _, _, _ = take(3)
    if not tail:
        p, u, bo = take(3)
    if head:
        bo_a, bo_b, bo_c = take(3)
    if not tail:
        va, vb, vc = take(3)
        last, first, side = take(3)
        fix, taps = take(2)
    fill_taps(taps)

    strike, dip = lax.axis_index("strike"), lax.axis_index("dip")
    keep_up = jnp.where(strike > 0, 1.0, 0.0)
    keep_down = jnp.where(strike < lax.axis_size("strike") - 1, 1.0, 0.0)
    keep_left = jnp.where(dip > 0, 1.0, 0.0)
    keep_right = jnp.where(dip < lax.axis_size("dip") - 1, 1.0, 0.0)

    def halo(level, _):
        p[level + 1, OFF - 4 : OFF, :] = from_up[level, :, :] * keep_up
        p[level + 1, OFF + CX : OFF + CX + 4, :] = from_down[level, :, :] * keep_down
        return 0

    lax.fori_loop(start, stop, halo, 0, unroll=8)

    spot = lanes((CX, CY)) & 7
    low_half = spot < 4
    if head:

        def halo_u(pair, _):
            for half in range(2):
                here = slice(2 * half, 2 * half + 2)
                level = 2 * pair + half
                u[level, OFF - 2 : OFF, :] = from_up[LEV + pair, here, :] * keep_up
                u[level, OFF + CX : OFF + CX + 2, :] = from_down[LEV + pair, here, :] * keep_down
            return 0

        lax.fori_loop(0, LEV // 2, halo_u, 0, unroll=4)
        bo[OFF - 2 : OFF, :] = from_up[LEV + LEV // 2, 0:2, :] * keep_up
        bo[OFF + CX : OFF + CX + 2, :] = from_down[LEV + LEV // 2, 0:2, :] * keep_down
        mine = own[2 * GROUPS]
        bo_a[...] = jnp.where(low_half, from_left[2 * GROUPS] * keep_left, mine)
        bo_b[...] = jnp.where(low_half, mine, from_right[2 * GROUPS] * keep_right)
        bo_c[...] = mine
        for g in range(GROUPS):
            mine = own[GROUPS + g]
            va[g] = jnp.where(low_half, from_left[GROUPS + g] * keep_left, mine)
            vb[g] = jnp.where(low_half, mine, from_right[GROUPS + g] * keep_right)
            vc[g] = mine

    middle = (spot >= 2) & (spot < 6)
    fields = []
    for g in range(*blocks):
        mine = own[g]
        fields.append(jnp.where(low_half, from_left[g] * keep_left, mine))
        fields.append(jnp.where(low_half, mine, from_right[g] * keep_right))
        fields.append(mine)
    turn = lane_diff(jnp.concatenate(fields, axis=0), taps)
    fields = []
    for n, g in enumerate(range(*blocks)):
        at = 3 * n * CX
        new_a = va[g] - bo_a[...] * turn[at : at + CX]
        new_b = vb[g] - bo_b[...] * turn[at + CX : at + 2 * CX]
        new_c = vc[g] - bo_c[...] * turn[at + 2 * CX : at + 3 * CX]
        if not tail:
            va[g] = new_a
            vb[g] = new_b
            vc[g] = new_c
        fields.append(jnp.where(middle, new_a - new_c, 0.0))
        fields.append(jnp.where(middle, new_b - new_c, 0.0))
    turn = lane_diff(jnp.concatenate(fields, axis=0), taps)
    for n, g in enumerate(range(*blocks)):
        at = 2 * n * CX
        fix[g] = jnp.where(low_half, turn[at + CX : at + 2 * CX], turn[at : at + CX])

    def rims(level, _):
        for row in (OFF - 2, OFF + CX - 2):
            rows = slice(row, row + 4)
            grad = row_diff(p, level + 1, row - 2)[2:6, :]
            u[level, rows, :] = u[level, rows, :] - bo[rows, :] * grad
        return 0

    lax.fori_loop(start, stop, rims, 0, unroll=8)

    lane = lanes()
    edge = (lane < 4) | (lane >= CY - 4)
    group_of = lane >> 3

    def one(group, _):
        for b in range(BLOCKS):
            at = block(b)
            gain = bk[at, :]
            sides_gain = jnp.where(edge, gain, 0.0)
            spread = fix[group, at, :]
            packed = jnp.zeros((8, CY), F32)
            for j in range(16):
                level = group * 16 + j
                new_p = sides_gain * rolled(spread, -(8 * j + 4))
                if 0 < b < BLOCKS - 1:
                    new_p = p[level + 1, padded(b), :] - new_p
                else:
                    new_p = rest[level, block(min(b, 1)), :] - new_p
                    new_p = new_p - gain * row_diff(u, level, OFF + 8 * b)
                if deepest and j == 15:
                    here = jnp.where(group == GROUPS - 1, 1.0, 0.0)
                    new_p = new_p + here * inj[step, at, :]
                if tail:
                    fresh[j, at, :] = new_p
                else:
                    p[level + 1, padded(b), :] = new_p
                    packed = jnp.where(group_of == j, rolled(new_p, 8 * j + 4), packed)
                    if b == 0:
                        first[level, :, :] = new_p[0:4, :]
                    if b == BLOCKS - 1:
                        last[level, :, :] = new_p[4:8, :]
            if not tail:
                side[group, at, :] = packed
        if tail:
            copy = pltpu.make_async_copy(fresh, out.at[pl.ds(group * 16, 16)], sems.at[0])
            copy.start()
        return 0

    if tail:
        one(part, 0)
        if deepest:
            floor[...] = fresh[15]
        pltpu.make_async_copy(fresh, out.at[pl.ds(part * 16, 16)], sems.at[0]).wait()
    else:
        lax.fori_loop(0, GROUPS, one, 0)


def kept(*arrays):
    space = pltpu.MemorySpace.HBM
    return [pltpu.with_memory_space_constraint(x, space) for x in arrays]


def shaped(*shape):
    return jax.ShapeDtypeStruct(shape, F32)


def params(mib):
    return pltpu.CompilerParams(vmem_limit_bytes=mib << 20)


def cost(mib):
    return pl.CostEstimate(flops=20_000_000, bytes_accessed=mib << 20, transcendentals=0)


P_SHAPE = shaped(LEV + 2, ROWS, CY)
U_SHAPE = shaped(LEV, ROWS, CY)
V_SHAPE = shaped(LEV, CX, CY)
W_SHAPE = shaped(LEV + 2, CX, CY)
BO_SHAPE = shaped(ROWS, CY)
MAP = shaped(CX, CY)
TAPS = pltpu.VMEM((2 * CY, CY), jnp.bfloat16)
SIDE = shaped(GROUPS, CX, CY)
STRIP = shaped(LEV, 4, CY)


def prep(gravity, amp, owner, cell):
    return pl.pallas_call(
        prep_kernel,
        out_shape=(shaped(LEV, CY), shaped(8, CY)),
        in_specs=[ANY] * 4,
        out_specs=[VMEM] * 2,
        scratch_shapes=[
            pltpu.SMEM((LEV,), F32),
            pltpu.SMEM((STEPS, 8), F32),
            pltpu.SMEM((8,), jnp.int32),
            pltpu.SMEM((8,), jnp.int32),
            pltpu.SemaphoreType.DMA((4,)),
        ],
        compiler_params=params(4),
        name="prep",
    )(*kept(gravity, amp, owner, cell))


def load(bulk_t, buoy_t, bathy, p, u, v):
    wide = shaped(LEV + LEV // 2 + 1, 4, CY)
    return pl.pallas_call(
        load_kernel,
        out_shape=(
            P_SHAPE, U_SHAPE, V_SHAPE, BO_SHAPE, MAP, wide, wide,
            shaped(2 * GROUPS + 1, CX, CY),
        ),
        in_specs=[ANY] * 6,
        out_specs=[VMEM] * 8,
        scratch_shapes=[
            pltpu.SMEM((NCLASS,), F32),
            pltpu.SMEM((NCLASS,), F32),
            pltpu.VMEM((CX, CY), jnp.int32),
            pltpu.SemaphoreType.DMA((6,)),
        ],
        compiler_params=params(16),
        cost_estimate=cost(8),
        name="load",
    )(*kept(bulk_t, buoy_t, bathy, p, u, v))


def inner(sc, bk, bo, p, u, v, w):
    args = (sc, bk, bo, p, u, v) + (() if w is None else (w,))
    alias = {3: 0, 4: 1, 5: 2}
    if w is not None:
        alias[6] = 3
    return pl.pallas_call(
        functools.partial(inner_kernel, w is not None),
        out_shape=(P_SHAPE, U_SHAPE, V_SHAPE, W_SHAPE, shaped(LEV, 16, CY)),
        in_specs=[VMEM] * len(args),
        out_specs=[VMEM] * 5,
        scratch_shapes=[TAPS],
        input_output_aliases=alias,
        compiler_params=params(16),
        cost_estimate=cost(16),
        name="inner",
    )(*args)


def sensors(table):
    return pl.pallas_call(
        sensor_kernel,
        out_shape=shaped(STEPS, CX, CY),
        in_specs=[SMEM],
        out_specs=VMEM,
        compiler_params=params(4),
        name="sensors",
    )(table)


def outer(step, bk, inj, rest, own, up, down, left, right, p, u, bo, state):
    head = step == 0
    args = [bk, inj, rest, own, up, down, left, right, p, u, bo]
    shapes = [P_SHAPE, U_SHAPE, BO_SHAPE]
    alias = {8: 0, 9: 1, 10: 2}
    if head:
        shapes += [MAP, MAP, MAP, SIDE, SIDE, SIDE]
    else:
        args += list(state)
        shapes += [SIDE, SIDE, SIDE]
        alias.update({14: 3, 15: 4, 16: 5})
    shapes += [STRIP, STRIP, SIDE]
    return pl.pallas_call(
        functools.partial(outer_kernel, step, None),
        out_shape=tuple(shapes),
        in_specs=[VMEM] * len(args),
        out_specs=[VMEM] * len(shapes),
        scratch_shapes=[pltpu.VMEM((GROUPS, CX, CY), F32), TAPS],
        input_output_aliases=alias,
        compiler_params=params(20),
        cost_estimate=cost(12),
        name="outer",
    )(*args)


def finish(part, bk, inj, rest, own, up, down, left, right, p, u, bo, state, out):
    args = [bk, inj, rest, own, up, down, left, right, p, u, bo, *state]
    in_specs = [VMEM] * len(args)
    shapes = [P_SHAPE, U_SHAPE, BO_SHAPE, V_SHAPE]
    specs = [VMEM] * 3 + [ANY]
    alias = {8: 0, 9: 1, 10: 2}
    if out is None:
        shapes.append(MAP)
        specs.append(VMEM)
    else:
        alias[len(args)] = 3
        args.append(out)
        in_specs.append(ANY)
    return pl.pallas_call(
        functools.partial(outer_kernel, STEPS - 1, part),
        out_shape=tuple(shapes),
        in_specs=in_specs,
        out_specs=specs,
        scratch_shapes=[
            pltpu.VMEM((GROUPS, CX, CY), F32),
            TAPS,
            pltpu.VMEM((16, CX, CY), F32),
            pltpu.SemaphoreType.DMA((1,)),
        ],
        input_output_aliases=alias,
        compiler_params=params(16),
        cost_estimate=cost(6),
        name="finish",
    )(*args)


def factor_kernel(gram, out):
    lane = lax.broadcasted_iota(jnp.int32, (8, PROBES), 1)
    row = lax.broadcasted_iota(jnp.int32, (8, PROBES), 0)
    rows = [gram[8 * i : 8 * i + 8, :] for i in range(PROBES // 8)]
    for k in range(PROBES // 8):
        strip = rows[k]
        cols = [jnp.broadcast_to(strip[:, 8 * k + t : 8 * k + t + 1], (8, PROBES)) for t in range(8)]
        scale = jnp.zeros((8, PROBES), F32)
        for t in range(8):
            pivot = jnp.broadcast_to(cols[t][t : t + 1, :], (8, PROBES))
            root = lax.rsqrt(pivot)
            root = root * (1.5 - 0.5 * pivot * root * root)
            scale = jnp.where(row == t, root, scale)
            share = jnp.where(row > t, cols[t] * (root * root), 0.0)
            for s in range(t + 1, 8):
                cols[s] = cols[s] - share * jnp.broadcast_to(cols[s][t : t + 1, :], (8, PROBES))
            strip = strip - share * jnp.broadcast_to(strip[t : t + 1, :], (8, PROBES))
        strip = jnp.where(lane >= 8 * k + row, strip * scale, 0.0)
        out[8 * k : 8 * k + 8, :] = strip
        if k < PROBES // 8 - 1:
            drop = lax.dot_general(strip, strip, (((0,), (0,)), ((), ())),
                precision=lax.Precision.HIGHEST, preferred_element_type=F32)
            for m in range(k + 1, PROBES // 8):
                rows[m] = rows[m] - drop[8 * m : 8 * m + 8, :]

def factor(gram):
    return pl.pallas_call(
        factor_kernel,
        out_shape=shaped(PROBES, PROBES),
        in_specs=[VMEM],
        out_specs=VMEM,
        compiler_params=params(4),
        name="factor",
    )(gram)


def ring(x, axis, by):
    n = lax.axis_size(axis)
    return lax.ppermute(x, axis, [(i, (i + by) % n) for i in range(n)])


def swap(x, axis, bit):
    n = lax.axis_size(axis)
    return lax.ppermute(x, axis, [(i, i ^ bit) for i in range(n)])


def weighted_gram(probes, weight):
    flat = probes.reshape(PROBES, CX * CY)
    rest = flat.astype(F32) * weight.reshape(1, CX * CY)
    parts = []
    for _ in range(3):
        part = lax.reduce_precision(rest, 8, 7)
        rest = rest - part
        parts.append(part.astype(jnp.bfloat16))
    both = jnp.concatenate(parts, axis=0)
    sums = lax.dot_general(
        flat, both, (((1,), (1,)), ((), ())), preferred_element_type=F32
    )
    return sums[:, :PROBES] + sums[:, PROBES : 2 * PROBES] + sums[:, 2 * PROBES :]


def body(
    pressure,
    strike_vel,
    dip_vel,
    bathy_class,
    bulk_table,
    buoy_table,
    gravity,
    sensor_amp,
    sensor_owner,
    sensor_cell,
    probe_kernel,
):
    strikes, dips = lax.axis_size("strike"), lax.axis_size("dip")
    sc, table = prep(gravity, sensor_amp, sensor_owner[:, 0], sensor_cell)
    for bit in (1, 2, 4):
        table = table + swap(table, "dip", bit)
    inj = sensors(table)

    p, u, v, bo, bk, last, first, side = load(
        bulk_table, buoy_table, bathy_class, pressure, strike_vel, dip_vel
    )
    w = None
    state = None
    for step in range(STEPS):
        up, down = ring(last, "strike", 1), ring(first, "strike", -1)
        left, right = ring(side, "dip", 1), ring(side, "dip", -1)
        p, u, v, w, rest = inner(sc, bk, bo, p, u, v, w)
        if step == STEPS - 1:
            break
        res = outer(step, bk, inj, rest, side, up, down, left, right, p, u, bo, state)
        p, u, bo = res[:3]
        if step == 0:
            state = res[3:9]
        else:
            state = state[:3] + res[3:6]
        last, first, side = res[-3:]

    def piece(part, p, u, bo, out):
        return finish(
            part, bk, inj, rest, side, up, down, left, right, p, u, bo, state, out
        )

    p, u, bo, out, seafloor = piece(GROUPS - 1, p, u, bo, None)
    cells = CX * CY
    total_cells = cells * strikes * dips
    scale = 1.0 / math.sqrt(total_cells)
    gram = weighted_gram(probe_kernel, (seafloor * scale) ** 2)
    gram = gram + swap(gram, "dip", 1)
    part = GROUPS - 2
    for axis, stride in (("dip", 2), ("strike", 1), ("strike", 4)):
        pieces = [swap(gram, axis, stride * bits) for bits in (1, 2, 3)]
        gram, p = lax.optimization_barrier((gram, p))
        p, u, bo, out = piece(part, p, u, bo, out)
        part -= 1
        *pieces, p = lax.optimization_barrier((*pieces, p))
        gram = gram + sum(pieces)
    return (out, factor(gram))


def solution(mesh):
    return jax.shard_map(
        body,
        mesh=mesh,
        in_specs=(
            P(None, "strike", "dip"),
            P(None, "strike", "dip"),
            P(None, "strike", "dip"),
            P("strike", "dip"),
            P(),
            P(),
            P(),
            P(None, ("strike", "dip")),
            P(("strike", "dip"), None),
            P(("strike", "dip")),
            P(None, "strike", "dip"),
        ),
        out_specs=(P(None, "strike", "dip"), P()),
        check_vma=False,
    )
```
